256 devices in a mesh: spec: 16 (over x, z_lo, core), neuron: 16 (over z_hi, y).
Axes of the slice: x: 4, y: 4, z: 8 (z_hi: 4, z_lo: 2; z = z_hi * 2 + z_lo), core: 2. Of those that a mesh axis runs over, the one named last changes fastest.
Arguments:
- center: float32 [128, 8192], P('spec', 'neuron'), may hold values from -6 to 6
- radius: float32 [128, 8192], P('spec', 'neuron'), may hold values from 0.002 to 0.02
- weight: float32 [4096, 8192], P('neuron'), may hold values from -0.0625 to 0.0625
- bias: float32 [4096], P('neuron'), may hold values from -3 to 3
- out_weight: float32 [1000, 4096], P(None, 'neuron'), may hold values from -0.09375 to 0.09375
- masks: int32 [128, 4096], P(None, 'neuron'), may hold values from 0 to 2
- image_labels: int32 [128], replicated, may hold values from 0 to 999
- runner_up: int32 [8192], P('spec'), may hold values from 0 to 999
- spec_image: int32 [8192], P('spec'), may hold values from 0 to 127
Outputs:
- input_coeffs: float32 [8192, 8192], P('spec', 'neuron')
- margin_bounds: float32 [8192], P('spec')
The draws below stay inside these ranges and needn't reach their ends.
All inputs are finite; a program needn't handle non-finite values.
Results may differ from the reference program's by a relative error of at most 0.000098.
Values sent between devices are 32-bit elements; how exact they have to be, the bound alone decides.
A program may use at most 128 MiB of HBM per device.

```python
import math
import jax
import jax.numpy as jnp
from jax import lax

D = 8192
H = 4096
CLASSES = 1000
B_TOTAL = 128
SPECS = 8192


def touch_ends(drawn, stream_key, smallest, high):
    longest = drawn.shape.index(max(drawn.shape))
    spots = []
    for shift in (0, 1):
        where = [jax.random.randint(jax.random.fold_in(stream_key, axis), (), 0, length) for axis, length in enumerate(drawn.shape)]
        where[longest] = (where[longest] + shift) % drawn.shape[longest]
        spots.append(tuple(where))
    return drawn.at[spots[0]].set(smallest).at[spots[1]].set(high)


def steps_of(key, dims, pieces, smallest, top_value):
    def one(axis_at, blocks):
        steps = jax.random.uniform(jax.random.fold_in(jax.random.fold_in(key, 6), axis_at), (blocks,), jnp.float32, smallest / len(pieces), top_value / len(pieces))
        return jnp.repeat(jnp.exp(steps), dims[axis_at] // blocks).reshape((-1,) + (1,) * (len(dims) - axis_at - 1))

    loudness = one(*pieces[0])
    for cut in pieces[1:]:
        loudness = loudness * one(*cut)
    return loudness


def gaussian(rng, dims, spread, bound, shards=(), kind=jnp.bfloat16):
    result = spread * jax.random.normal(rng, dims, jnp.float32)
    if shards:
        result = result * steps_of(rng, dims, shards, -0.22, 0.18)
    return jnp.clip(result, -bound, bound).astype(kind)


def setup_inputs(seed: int = 0) -> dict:
    splits = jax.random.split(jax.random.key(seed), 10)
    return {
        "center": gaussian(splits[0], (B_TOTAL, D), 1.0, 6.0, ((0, 16), (1, 16)), jnp.float32),
        "radius": jnp.clip(jnp.exp(math.log(0.02) - 2.30258502 * jax.random.uniform(splits[1], (B_TOTAL, D), jnp.float32) ** steps_of(splits[1], (B_TOTAL, D), ((0, 16), (1, 16)), -0.2, 0.2)), 0.002, 0.02),
        "weight": gaussian(splits[2], (H, D), D ** -0.5, 0.0625, ((0, 16),), jnp.float32),
        "bias": gaussian(splits[3], (H,), 0.5, 3.0, ((0, 16),), jnp.float32),
        "out_weight": gaussian(splits[4], (CLASSES, H), H ** -0.5, 0.09375, ((1, 16),), jnp.float32),
        "masks": touch_ends(jax.random.randint(splits[5], (B_TOTAL, H), 0, 3), jax.random.fold_in(splits[5], 1), 0, 2).astype(jnp.int32),
        "image_labels": touch_ends(jax.random.randint(splits[6], (B_TOTAL,), 0, CLASSES), jax.random.fold_in(splits[6], 1), 0, CLASSES - 1).astype(jnp.int32),
        "runner_up": touch_ends(jax.random.randint(splits[7], (SPECS,), 0, CLASSES), jax.random.fold_in(splits[7], 1), 0, CLASSES - 1).astype(jnp.int32),
        "spec_image": touch_ends(jax.random.randint(splits[8], (SPECS,), 0, B_TOTAL), jax.random.fold_in(splits[8], 1), 0, B_TOTAL - 1).astype(jnp.int32),
    }


def relax(pre_center, pre_radius, masks):
    upper = pre_center + pre_radius
    lower = pre_center - pre_radius
    slope = jnp.clip(upper / (upper - lower), 0.0, 1.0)
    slopes = jnp.where(masks == 1, jnp.ones_like(slope), jnp.where(masks == 2, slope, jnp.zeros_like(slope)))
    offsets = jnp.where(masks == 2, slope * lower, jnp.zeros_like(slope))
    return slopes, offsets


def reference(center, radius, weight, bias, out_weight, masks, image_labels, runner_up, spec_image):
    highest = lax.Precision.HIGHEST
    pre_center = jnp.dot(center, weight.T, precision=highest) + bias
    pre_radius = jnp.dot(radius, jnp.abs(weight).T, precision=highest)
    slopes, offsets = relax(pre_center, pre_radius, masks)
    true_class = image_labels[spec_image]
    spec_coeff = out_weight[true_class] - out_weight[runner_up]
    scaled = spec_coeff * slopes[spec_image]
    relax_term = -jnp.sum(jnp.minimum(spec_coeff, 0.0) * offsets[spec_image], axis=1) + jnp.sum(scaled * bias, axis=1)
    input_coeffs = jnp.dot(scaled, weight, precision=highest)
    input_term = jnp.sum(input_coeffs * center[spec_image] - jnp.abs(input_coeffs) * radius[spec_image], axis=1)
    return input_coeffs, input_term + relax_term
```

```python
import jax
import jax.numpy as jnp
from jax import lax
from jax.experimental import pallas as pl
from jax.experimental.pallas import tpu as pltpu
from jax.sharding import PartitionSpec as P

MESH = pl.DeviceIdType.MESH
F32, BF16 = jnp.float32, jnp.bfloat16


def split(v):
    hi = v.astype(BF16)
    return hi, (v - hi.astype(F32)).astype(BF16)


def dot(a, b):
    return lax.dot_general(a, b, (((1,), (0,)), ((), ())), preferred_element_type=F32)


def dot_t(a, b):
    return lax.dot_general(a, b, (((1,), (1,)), ((), ())), preferred_element_type=F32)


def sid(x, zl, c):
    return ((x + 4) % 4 * 2 + zl) * 2 + c


def nid(zh, y):
    return (zh + 4) % 4 * 4 + (y + 4) % 4


TILES = (
    (1, 0, 0, 0),
    (-1, 0, 0, 512),
    (0, 1, 0, 1024),
    (0, -1, 1, 1280),
    (1, 0, 1, 256),
    (-1, 0, 1, 768),
    (0, 0, 0, 1536),
    (0, 0, 1, 1792),
)
CLASS = ((0, 0), (2, 1), (0, 2), (2, 3))
N_SEM = 160


def kernel(
    center, radius, w, bias, ow, masks, labels, runner, simg, out, marg,
    wl, wb, owb, cb, ca, sa, sc, sh, sl, whi, wlo, sendb, recvb, crow, rrow, rel, eb, ob, mb, ss, rs, ls,
):
    s, n = lax.axis_index("spec"), lax.axis_index("neuron")
    x, zl, c = s // 4, s // 2 % 2, s % 2
    zh, y = n // 4, n % 4
    u = x * 2 + c

    started = []
    counter = [0]

    def take(k=1):
        counter[0] += k
        assert counter[0] <= N_SEM
        return counter[0] - k

    def send(src, dst, sem, dev):
        copy = pltpu.make_async_remote_copy(
            src_ref=src, dst_ref=dst, send_sem=ss.at[len(started)], recv_sem=rs.at[sem],
            device_id=dev, device_id_type=MESH,
        )
        copy.start()
        started.append(copy)

    def arrived(dst, sem):
        pltpu.make_async_copy(dst, dst, rs.at[sem]).wait()

    lc = [
        pltpu.make_async_copy(center, cb.at[y, zh, 0], ls.at[0]),
        pltpu.make_async_copy(radius, cb.at[y, zh, 1], ls.at[1]),
        pltpu.make_async_copy(ow, owb.at[0, 0:1000], ls.at[2]),
    ]
    for copy in lc:
        copy.start()
    wc = [
        pltpu.make_async_copy(w.at[:, pl.ds(i * 2048, 2048)], wl.at[:, pl.ds(i * 2048, 2048)], ls.at[3 + i])
        for i in range(4)
    ]
    for copy in wc:
        copy.start()

    peers = [(s, (n + d) % 16) for d in range(1, 16)]
    peers += [(sid(x + d, zl, c), n) for d in (1, 2, 3)]
    peers += [(sid(x, 1 - zl, c), n), (sid(x, zl, 1 - c), n)]
    peers += [(sid(x, 1 - zl, c), nid(zh + 2 * zl - 1, y + 2)), (sid(x, 1 - zl, c), nid(zh + 2, y))]
    barrier = pltpu.get_barrier_semaphore()
    for peer in peers:
        pl.semaphore_signal(barrier, inc=1, device_id=peer, device_id_type=MESH)
    pl.semaphore_wait(barrier, len(peers))

    lc[0].wait()
    lc[1].wait()
    cz, cy, cx = take(3), take(3), take(3)
    for d in (1, 2, 3):
        send(cb.at[y, zh], cb.at[y, zh], cz + d - 1, (s, nid(zh + d, y)))

    rows_o, rows_w = pl.ds(pl.multiple_of(120 * u, 8), 120), pl.ds(pl.multiple_of(32 * u, 32), 32)
    roles = [
        (sid(x, 0, c), zh + 2 * zl - 1, y + 2, 1 + 2 * zl),
        (sid(x, 1, c), zh + 2 * zl - 1, y + 2, 1 + 2 * zl),
        (sid(x, 1 - zl, c), zh + 2, y, 2),
    ]
    direct = {g: take(3) for g in "OAB"}
    for sd, zd, yd, j in roles:
        dev = (sd, nid(zd, yd))
        send(ow.at[rows_o], owb.at[j, rows_o], direct["O"] + j - 1, dev)
        send(ow.at[960:1000], owb.at[j, 960:1000], direct["O"] + j - 1, dev)
    for d in (1, 2, 3):
        send(cb.at[y, zh], ca.at[:, x, zl, c], cx + d - 1, (sid(x + d, zl, c), n))
    for sd, zd, yd, j in roles:
        dev = (sd, nid(zd, yd))
        for dy, dz, half, at in (TILES[0], TILES[1], TILES[2], TILES[3]):
            wide = 512 if dy else 256
            cols = pl.ds(pl.multiple_of(nid(zd + dz, yd + dy) * 512 + half * 256, 256), wide)
            send(w.at[rows_w, cols], wb.at[j - 1, rows_w, at : at + wide], direct["A"] + j - 1, dev)
    for sd, zd, yd, j in roles:
        dev = (sd, nid(zd, yd))
        cols = pl.ds(pl.multiple_of(nid(zd, yd) * 512, 512), 512)
        send(w.at[rows_w, cols], wb.at[j - 1, rows_w, 1536:2048], direct["B"] + j - 1, dev)

    def region(g, j, q, part=None):
        if g == "O":
            start, size = (0, 120) if part is None else ((0, 64), (64, 56))[part]
            return owb.at[j, pl.ds(pl.multiple_of(120 * q + start, 8), size)]
        start, size = (0, 32) if part is None else ((0, 16), (16, 16))[part]
        rows = pl.ds(pl.multiple_of(32 * q + start, 8), size)
        return wb.at[j - 1, rows, 0:1536] if g == "A" else wb.at[j - 1, rows, 1536:2048]

    left, right, sib = (sid(x - 1, zl, c), n), (sid(x + 1, zl, c), n), (sid(x, zl, 1 - c), n)
    ul, ur, uf = (x + 3) % 4 * 2 + c, (x + 1) % 4 * 2 + c, (x + 2) % 4 * 2 + c
    sem = {(g, j): take(5) for g in "OAB" for j in (1, 2, 3)}

    def pass_own(g, j):
        if g == "O":
            arrived(owb.at[j, 0:160], direct[g] + j - 1)
        else:
            arrived(region(g, j, u), direct[g] + j - 1)
        send(region(g, j, u), region(g, j, u), sem[g, j], right)
        send(region(g, j, u), region(g, j, u), sem[g, j] + 1, left)
        send(region(g, j, u), region(g, j, u), sem[g, j] + 4, sib)

    def pass_near(g, j):
        arrived(region(g, j, ul), sem[g, j])
        send(region(g, j, ul, 0), region(g, j, ul, 0), sem[g, j] + 2, right)
        send(region(g, j, ul), region(g, j, ul), sem[g, j] + 4, sib)
        arrived(region(g, j, ur), sem[g, j] + 1)
        send(region(g, j, ur, 1), region(g, j, ur, 1), sem[g, j] + 3, left)
        send(region(g, j, ur), region(g, j, ur), sem[g, j] + 4, sib)

    def pass_far(g, j):
        arrived(region(g, j, uf, 0), sem[g, j] + 2)
        arrived(region(g, j, uf, 1), sem[g, j] + 3)
        send(region(g, j, uf), region(g, j, uf), sem[g, j] + 4, sib)

    def whole(g, j):
        if g == "O":
            arrived(owb.at[j, 0:480], sem[g, j] + 4)
        elif g == "A":
            arrived(wb.at[j - 1, 0:128, 0:1536], sem[g, j] + 4)
        else:
            arrived(wb.at[j - 1, 0:128, 1536:2048], sem[g, j] + 4)

    for d in (1, 2, 3):
        arrived(cb.at[y, nid(zh - d, 0) // 4], cz + d - 1)
    for d in (1, 2, 3):
        send(cb.at[y], cb.at[y], cy + d - 1, (s, nid(zh, y + d)))

    img = jnp.transpose(jnp.broadcast_to(simg[...], (128, 512)))
    run = jnp.transpose(jnp.broadcast_to(runner[...], (128, 512)))[:, 0:1]
    picked = img == lax.broadcasted_iota(jnp.int32, (512, 128), 1)
    ob[...] = jnp.where(picked, 1.0, 0.0).astype(BF16)
    lab = jnp.sum(jnp.where(picked, labels[...].astype(F32), 0.0), axis=1, keepdims=True).astype(jnp.int32)
    for k in range(8):
        ids = lax.broadcasted_iota(jnp.int32, (512, 128), 1) + k * 128
        e = jnp.where(ids == lab, 1.0, 0.0) - jnp.where(ids == run, 1.0, 0.0)
        eb[:, k * 128 : (k + 1) * 128] = e.astype(BF16)
    for j in range(4):
        owb[j, 1000:1024, :] = jnp.zeros((24, 256), F32)

    for copy in wc:
        copy.wait()

    def pre_row(yy, carry):
        def body(k, carry):
            pc, pr = carry
            at = pl.multiple_of((k * 4 + yy) * 512, 512)
            chi, clo = split(cb[yy, k, 0])
            rhi, rlo = split(cb[yy, k, 1])
            cc, rr = jnp.concatenate([chi, clo], axis=0), jnp.concatenate([rhi, rlo], axis=0)
            wt = wl[:, pl.ds(at, 512)]
            thi, tlo = split(wt)
            pc = pc + dot_t(cc, thi) + dot_t(cc, tlo)
            thi, tlo = split(jnp.abs(wt))
            pr = pr + dot_t(rr, thi) + dot_t(rr, tlo)
            return pc, pr

        return lax.fori_loop(0, 4, body, carry)

    zero = jnp.zeros((16, 256), F32)
    carry = pre_row(y, (zero, zero))
    for j in (1, 2, 3):
        pass_own("O", j)
    for d in (1, 2, 3):
        arrived(cb.at[(y + 4 - d) % 4], cy + d - 1)
        carry = pre_row((y + 4 - d) % 4, carry)
    pc = carry[0][0:8] + carry[0][8:16] + bias[...]
    pr = carry[1][0:8] + carry[1][8:16]
    upper, lower = pc + pr, pc - pr
    slope = jnp.clip(upper / (upper - lower), 0.0, 1.0)
    m = masks[pl.ds(pl.multiple_of(8 * s, 8), 8), :]
    sa[0, x, zl, c] = jnp.where(m == 1, 1.0, jnp.where(m == 2, slope, 0.0))
    sa[4, x, zl, c] = jnp.where(m == 2, slope * lower, 0.0)
    sj = take(3)
    for j in (1, 2, 3):
        dy, dz = CLASS[j]
        send(sa.at[0, x, zl, c], sa.at[j, x, zl, c], sj + j - 1, (s, nid(zh - dz, y - dy)))

    for j in (1, 2, 3):
        pass_near("O", j)

    def gather_x(buf, base):
        for d in (1, 2, 3):
            arrived(buf.at[:, (x + 4 - d) % 4, zl, c], base + d - 1)

    cl, cc = take(), take()
    own = cb[y, zh]
    ca[:, x, zl, c] = own
    gather_x(ca, cx)
    send(ca.at[:, :, zl, c], ca.at[:, :, zl, c], cl, (sid(x, 1 - zl, c), n))

    for j in (1, 2, 3):
        arrived(sa.at[j, x, zl, c], sj + j - 1)
    sx, sz, sk = take(3), take(), take()
    for d in (1, 2, 3):
        send(sa.at[:, x, zl, c], sa.at[:, x, zl, c], sx + d - 1, (sid(x + d, zl, c), n))
    for j in (1, 2, 3):
        pass_far("O", j)
    for j in (1, 2, 3):
        pass_own("A", j)
    gather_x(sa, sx)
    send(sa.at[:, :, zl, c], sa.at[:, :, zl, c], sz, (sid(x, 1 - zl, c), n))
    arrived(ca.at[:, :, 1 - zl, c], cl)
    send(ca.at[:, :, :, c], ca.at[:, :, :, c], cc, sib)

    lc[2].wait()
    for j in (1, 2, 3):
        whole("O", j)

    def coeff(j, _):
        hi, lo = split(owb[j])
        e = eb[...]
        sc[j] = dot(e, hi) + dot(e, lo)
        return 0

    lax.fori_loop(0, 4, coeff, 0)

    for j in (1, 2, 3):
        pass_near("A", j)
    arrived(sa.at[:, :, 1 - zl, c], sz)
    send(sa.at[:, :, :, c], sa.at[:, :, :, c], sk, sib)
    for j in (1, 2, 3):
        pass_own("B", j)
    for j in (1, 2, 3):
        pass_far("A", j)
    arrived(sa.at[:, :, :, 1 - c], sk)

    def scale(j, _):
        hi, lo = split(sa[j].reshape(128, 256))
        o = ob[...]
        v = sc[j] * (dot(o, hi) + dot(o, lo))
        hi, lo = split(v)
        sh[j] = hi
        sl[j] = lo
        return 0

    lax.fori_loop(0, 4, scale, 0)
    hi, lo = split(sa[4].reshape(128, 256))
    off = dot(ob[...], hi) + dot(ob[...], lo)
    t = (sh[0].astype(F32) + sl[0].astype(F32)) * bias[...] - jnp.minimum(sc[0], 0.0) * off
    rel[...] = t[:, 0:128] + t[:, 128:256]

    for j in (1, 2, 3):
        whole("A", j)

    def tile(k):
        dy, dz, half, at = TILES[k]
        cols = pl.ds(pl.multiple_of(nid(zh + dz, y + dy) * 512 + half * 256, 256), 256)
        for j in range(4):
            hi, lo = split(wl[:, cols] if j == 0 else wb[j - 1, :, at : at + 256])
            whi[j * 256 : (j + 1) * 256, :] = hi
            wlo[j * 256 : (j + 1) * 256, :] = lo
        a = jnp.concatenate([sh[j] for j in range(4)], axis=1)
        b = jnp.concatenate([sl[j] for j in range(4)], axis=1)
        sendb[k] = dot(a, whi[...]) + dot(b, whi[...]) + dot(a, wlo[...])

    rt = take(6)
    for k in range(6):
        tile(k)
        dy, dz, _, _ = TILES[k]
        send(sendb.at[k], recvb.at[k], rt + k, (s, nid(zh + dz, y + dy)))
        if k < 3:
            pass_near("B", k + 1)
        else:
            pass_far("B", k - 2)

    arrived(ca.at[:, :, :, 1 - c], cc)
    for which, dst in ((0, crow), (1, rrow)):
        hi, lo = split(ca[which].reshape(128, 512))
        dst[...] = dot(ob[...], hi) + dot(ob[...], lo)
    for j in (1, 2, 3):
        whole("B", j)
    tile(6)
    tile(7)

    for half, ks in ((0, (0, 1, 2)), (1, (4, 5, 3))):
        cols = slice(half * 256, half * 256 + 256)
        v = sendb[6 + half]
        for k in ks:
            arrived(recvb.at[k], rt + k)
            v = v + recvb[k]
        out[:, cols] = v
        t = v * crow[:, cols] - jnp.abs(v) * rrow[:, cols]
        rel[...] += t[:, 0:128] + t[:, 128:256]

    mb[n] = jnp.sum(jnp.transpose(rel[...]), axis=0, keepdims=True)
    ms = take(15)
    for d in range(1, 16):
        send(mb.at[n], mb.at[n], ms + d - 1, (s, (n + d) % 16))
    for d in range(1, 16):
        arrived(mb.at[(n + 16 - d) % 16], ms + d - 1)
    marg[...] = jnp.sum(mb[...], axis=0)

    for copy in started:
        copy.wait_send()


def local(center, radius, weight, bias, out_weight, masks, image_labels, runner_up, spec_image):
    vmem, hbm = pl.BlockSpec(memory_space=pltpu.VMEM), pl.BlockSpec(memory_space=pl.ANY)
    coeffs, margins = pl.pallas_call(
        kernel,
        out_shape=(jax.ShapeDtypeStruct((512, 512), F32), jax.ShapeDtypeStruct((1, 512), F32)),
        in_specs=[hbm, hbm, hbm, vmem, hbm, vmem, vmem, vmem, vmem],
        out_specs=(vmem, vmem),
        scratch_shapes=[
            pltpu.VMEM((256, 8192), F32),
            pltpu.VMEM((3, 256, 2048), F32),
            pltpu.VMEM((4, 1024, 256), F32),
            pltpu.VMEM((4, 4, 2, 8, 512), F32),
            pltpu.VMEM((2, 4, 2, 2, 8, 512), F32),
            pltpu.VMEM((5, 4, 2, 2, 8, 256), F32),
            pltpu.VMEM((4, 512, 256), F32),
            pltpu.VMEM((4, 512, 256), BF16),
            pltpu.VMEM((4, 512, 256), BF16),
            pltpu.VMEM((1024, 256), BF16),
            pltpu.VMEM((1024, 256), BF16),
            pltpu.VMEM((8, 512, 256), F32),
            pltpu.VMEM((6, 512, 256), F32),
            pltpu.VMEM((512, 512), F32),
            pltpu.VMEM((512, 512), F32),
            pltpu.VMEM((512, 128), F32),
            pltpu.VMEM((512, 1024), BF16),
            pltpu.VMEM((512, 128), BF16),
            pltpu.VMEM((16, 1, 512), F32),
            pltpu.SemaphoreType.DMA((N_SEM,)),
            pltpu.SemaphoreType.DMA((N_SEM,)),
            pltpu.SemaphoreType.DMA((8,)),
        ],
        compiler_params=pltpu.CompilerParams(
            collective_id=0, has_side_effects=True, vmem_limit_bytes=60 * 1024 * 1024
        ),
        name="bounds",
    )(
        center,
        radius,
        weight,
        bias.reshape(1, 256),
        out_weight,
        masks,
        image_labels.reshape(1, 128),
        runner_up.reshape(1, 512),
        spec_image.reshape(1, 512),
    )
    return coeffs, margins.reshape(512)


def solution(mesh):
    return jax.shard_map(
        local,
        mesh=mesh,
        in_specs=(
            P("spec", "neuron"),
            P("spec", "neuron"),
            P("neuron", None),
            P("neuron"),
            P(None, "neuron"),
            P(None, "neuron"),
            P(),
            P("spec"),
            P("spec"),
        ),
        out_specs=(P("spec", "neuron"), P("spec")),
        check_vma=False,
    )
```

```python
import jax
import jax.numpy as jnp
from jax import lax
from jax.experimental import pallas as pl
from jax.experimental.pallas import tpu as pltpu
from jax.sharding import PartitionSpec as P

MESH = pl.DeviceIdType.MESH
F32, BF16 = jnp.float32, jnp.bfloat16


def split(v):
    hi = v.astype(BF16)
    return hi, (v - hi.astype(F32)).astype(BF16)


def dot(a, b):
    return lax.dot_general(a, b, (((1,), (0,)), ((), ())), preferred_element_type=F32)


def dot_t(a, b):
    return lax.dot_general(a, b, (((1,), (1,)), ((), ())), preferred_element_type=F32)


def sid(x, zl, c):
    return ((x + 4) % 4 * 2 + zl) * 2 + c


def nid(zh, y):
    return (zh + 4) % 4 * 4 + (y + 4) % 4


TILES = ((1, 0, 0), (-1, 0, 0), (0, 1, 0), (0, -1, 1), (1, 0, 1), (-1, 0, 1), (0, 0, 0), (0, 0, 1))
SPAN = {"A": (0, 3), "B": (3, 6), "C": (6, 8)}
CLASS = ((0, 0), (2, 1), (0, 2), (2, 3))
N_SEND, N_RECV = 130, 130


def kernel(
    center, radius, w, bias, ow, masks, labels, runner, simg, out, marg,
    wl, wb, owb, cb, ca, sa, sc, sh, sl, whi, wlo, sendb, recvb, outb, crow, rrow, rel, eb, ob, mb, ss, rs, ls,
):
    s, n = lax.axis_index("spec"), lax.axis_index("neuron")
    x, zl, c = s // 4, s // 2 % 2, s % 2
    zh, y = n // 4, n % 4

    started = []
    counter = [0]

    def take(k=1):
        counter[0] += k
        assert counter[0] <= N_RECV
        return counter[0] - k

    def send(src, dst, sem, dev):
        copy = pltpu.make_async_remote_copy(
            src_ref=src, dst_ref=dst, send_sem=ss.at[len(started)], recv_sem=rs.at[sem],
            device_id=dev, device_id_type=MESH,
        )
        copy.start()
        started.append(copy)

    def arrived(dst, sem):
        pltpu.make_async_copy(dst, dst, rs.at[sem]).wait()

    lc = [
        pltpu.make_async_copy(center, cb.at[y, zh, 0], ls.at[0]),
        pltpu.make_async_copy(radius, cb.at[y, zh, 1], ls.at[1]),
        pltpu.make_async_copy(ow, owb.at[0, 0:1000], ls.at[2]),
    ]
    for copy in lc:
        copy.start()
    wc = [
        pltpu.make_async_copy(w.at[:, pl.ds(i * 2048, 2048)], wl.at[:, pl.ds(i * 2048, 2048)], ls.at[3 + i])
        for i in range(4)
    ]
    for copy in wc:
        copy.start()

    right, left, far = (sid(x + 1, zl, c), n), (sid(x - 1, zl, c), n), (sid(x + 2, zl, c), n)
    pair, sib = (sid(x, 1 - zl, c), n), (sid(x, zl, 1 - c), n)
    near = (sid(x, 1 - zl, c), nid(zh + 2 * zl - 1, y + 2))
    across = (sid(x, 1 - zl, c), nid(zh + 2, y))
    peers = [(s, (n + d) % 16) for d in range(1, 16)] + [right, left, far, pair, sib, near, across]
    barrier = pltpu.get_barrier_semaphore()
    for peer in peers:
        pl.semaphore_signal(barrier, inc=1, device_id=peer, device_id_type=MESH)
    pl.semaphore_wait(barrier, len(peers))

    lc[0].wait()
    lc[1].wait()
    cz, cy, cx = take(3), take(3), take(3)
    for d in (1, 2, 3):
        send(cb.at[y, zh], cb.at[y, zh], cz + d - 1, (s, nid(zh + d, y)))

    j_in, j_out = 3 - 2 * zl, 1 + 2 * zl
    order = (j_in, 2, j_out)
    groups = ("O", "A", "B", "C")
    base = {g: take(4 + 15) for g in groups}

    def part(g, j, q, which=None):
        if g == "O":
            start, size = ((0, 120), (0, 64), (64, 56))[0 if which is None else which + 1]
            return owb.at[j, pl.ds(pl.multiple_of(480 * c + 120 * q + start, 8), size)]
        start, size = ((0, 32), (0, 16), (16, 16))[0 if which is None else which + 1]
        lo, hi = SPAN[g]
        rows = pl.ds(pl.multiple_of(128 * c + 32 * q + start, 8), size)
        return wb.at[j - 1, rows, lo * 256 : hi * 256]

    def half_w(g, h):
        lo, hi = SPAN[g]
        return wb.at[1, pl.ds(pl.multiple_of(128 * c + 32 * x + 16 * h, 8), 16), lo * 256 : hi * 256]

    def half_o(h):
        start = 480 * c + 120 * x
        first = pl.ds(pl.multiple_of(start + 80 * h, 8), 40)
        second = pl.ds(pl.multiple_of(jnp.where(h == 0, start + 40, 960), 8), 40)
        return first, second

    def fetch(g):
        if g == "O":
            rows = pl.ds(pl.multiple_of(480 * c + 120 * x, 8), 120)
            send(ow.at[rows], owb.at[j_out, rows], base[g], near)
            send(ow.at[960:1000], owb.at[j_out, 960:1000], base[g], near)
            for rows in half_o(1 - zl):
                send(ow.at[rows], owb.at[2, rows], base[g] + 1, across)
            return
        lo, hi = SPAN[g]
        for dev, zd, yd, j, start, size in (
            (near, zh + 2 * zl - 1, y + 2, j_out, 0, 32),
            (across, zh + 2, y, 2, 16 * (1 - zl), 16),
        ):
            rows = pl.ds(pl.multiple_of(128 * c + 32 * x + start, 8), size)
            sem = base[g] + (0 if size == 32 else 1)
            k = lo
            while k < hi:
                dy, dz, half = TILES[k]
                wide = 512 if k == 6 else 256
                cols = pl.ds(pl.multiple_of(nid(zd + dz, yd + dy) * 512 + half * 256, 256), wide)
                send(w.at[rows, cols], wb.at[j - 1, rows, k * 256 : k * 256 + wide], sem, dev)
                k += wide // 256

    def ring(g, j):
        send(part(g, j, x), part(g, j, x), base[g] + 4 + 5 * (j - 1), right)
        send(part(g, j, x), part(g, j, x), base[g] + 5 + 5 * (j - 1), left)

    def pass_pair(g):
        if g == "O":
            arrived(owb.at[j_in, 0:160], base[g])
            send(part(g, j_in, x), part(g, j_in, x), base[g] + 2, pair)
            send(owb.at[j_in, 960:1000], owb.at[j_in, 960:1000], base[g] + 2, pair)
            arrived(owb.at[2, 0:80], base[g] + 1)
            for rows in half_o(zl):
                send(owb.at[2, rows], owb.at[2, rows], base[g] + 3, pair)
        else:
            arrived(part(g, j_in, x), base[g])
            send(part(g, j_in, x), part(g, j_in, x), base[g] + 2, pair)
            arrived(half_w(g, zl), base[g] + 1)
            send(half_w(g, zl), half_w(g, zl), base[g] + 3, pair)
        ring(g, j_in)

    def pass_own(g):
        if g == "O":
            arrived(owb.at[2, 0:80], base[g] + 3)
            ring(g, 2)
            arrived(owb.at[j_out, 0:160], base[g] + 2)
        else:
            arrived(half_w(g, 1 - zl), base[g] + 3)
            ring(g, 2)
            arrived(part(g, j_out, x), base[g] + 2)
        ring(g, j_out)

    xl, xr, xf = (x + 3) % 4, (x + 1) % 4, (x + 2) % 4

    def pass_near(g):
        for j in order:
            arrived(part(g, j, xl), base[g] + 4 + 5 * (j - 1))
            send(part(g, j, xl, 0), part(g, j, xl, 0), base[g] + 6 + 5 * (j - 1), right)
            arrived(part(g, j, xr), base[g] + 5 + 5 * (j - 1))
            send(part(g, j, xr, 1), part(g, j, xr, 1), base[g] + 7 + 5 * (j - 1), left)

    def core_half(g, j, cc):
        if g == "O":
            return owb.at[j, pl.ds(pl.multiple_of(480 * cc, 8), 480)]
        lo, hi = SPAN[g]
        return wb.at[j - 1, pl.ds(pl.multiple_of(128 * cc, 8), 128), lo * 256 : hi * 256]

    def pass_far(g):
        for j in order:
            arrived(part(g, j, xf, 0), base[g] + 6 + 5 * (j - 1))
            arrived(part(g, j, xf, 1), base[g] + 7 + 5 * (j - 1))
            send(core_half(g, j, c), core_half(g, j, c), base[g] + 8 + 5 * (j - 1), sib)

    def whole(g):
        for j in (1, 2, 3):
            arrived(core_half(g, j, 1 - c), base[g] + 8 + 5 * (j - 1))

    fetch("O")
    for d, dev in ((1, right), (2, far), (3, left)):
        send(cb.at[y, zh], ca.at[:, x, zl, c], cx + d - 1, dev)
    for d in (1, 2, 3):
        arrived(cb.at[y, (zh + 4 - d) % 4], cz + d - 1)
    for d in (1, 2, 3):
        send(cb.at[y], cb.at[y], cy + d - 1, (s, nid(zh, y + d)))
    fetch("A")

    img = jnp.transpose(jnp.broadcast_to(simg[...], (128, 512)))
    run = jnp.transpose(jnp.broadcast_to(runner[...], (128, 512)))[:, 0:1]
    picked = img == lax.broadcasted_iota(jnp.int32, (512, 128), 1)
    ob[...] = jnp.where(picked, 1.0, 0.0).astype(BF16)
    lab = jnp.sum(jnp.where(picked, labels[...].astype(F32), 0.0), axis=1, keepdims=True).astype(jnp.int32)
    for k in range(8):
        ids = lax.broadcasted_iota(jnp.int32, (512, 128), 1) + k * 128
        e = jnp.where(ids == lab, 1.0, 0.0) - jnp.where(ids == run, 1.0, 0.0)
        eb[:, k * 128 : (k + 1) * 128] = e.astype(BF16)
    for j in range(4):
        owb[j, 1000:1024, :] = jnp.zeros((24, 256), F32)
    ca[:, x, zl, c] = cb[y, zh]

    for copy in wc:
        copy.wait()

    def pre_row(yy, carry):
        def body(k, carry):
            pc, pr = carry
            at = pl.multiple_of((k * 4 + yy) * 512, 512)
            chi, clo = split(cb[yy, k, 0])
            rhi, rlo = split(cb[yy, k, 1])
            cc, rr = jnp.concatenate([chi, clo], axis=0), jnp.concatenate([rhi, rlo], axis=0)
            wt = wl[:, pl.ds(at, 512)]
            thi, tlo = split(wt)
            pc = pc + dot_t(cc, thi) + dot_t(cc, tlo)
            thi, tlo = split(jnp.abs(wt))
            pr = pr + dot_t(rr, thi) + dot_t(rr, tlo)
            return pc, pr

        return lax.fori_loop(0, 4, body, carry)

    pass_pair("O")
    zero = jnp.zeros((16, 256), F32)
    carry = pre_row(y, (zero, zero))
    pass_own("O")
    fetch("B")
    for d in (1, 2, 3):
        arrived(cb.at[(y + 4 - d) % 4], cy + d - 1)
        carry = pre_row((y + 4 - d) % 4, carry)
    pc = carry[0][0:8] + carry[0][8:16] + bias[...]
    pr = carry[1][0:8] + carry[1][8:16]
    upper, lower = pc + pr, pc - pr
    slope = jnp.clip(upper / (upper - lower), 0.0, 1.0)
    m = masks[pl.ds(pl.multiple_of(8 * s, 8), 8), :]
    sa[0, x, zl, c] = jnp.where(m == 1, 1.0, jnp.where(m == 2, slope, 0.0))
    sa[4, x, zl, c] = jnp.where(m == 2, slope * lower, 0.0)
    sj = take(3)
    for j in (1, 2, 3):
        dy, dz = CLASS[j]
        send(sa.at[0, x, zl, c], sa.at[j, x, zl, c], sj + j - 1, (s, nid(zh - dz, y - dy)))
    fetch("C")

    def gather_x(buf, sem):
        for d in (1, 2, 3):
            arrived(buf.at[:, (x + 4 - d) % 4, zl, c], sem + d - 1)

    pass_pair("A")
    pass_near("O")
    pass_own("A")
    cl, ck = take(), take()
    gather_x(ca, cx)
    send(ca.at[:, :, zl, c], ca.at[:, :, zl, c], cl, pair)
    for j in (1, 2, 3):
        arrived(sa.at[j, x, zl, c], sj + j - 1)
    sx, sz, sk = take(3), take(), take()
    for d, dev in ((1, right), (2, far), (3, left)):
        send(sa.at[:, x, zl, c], sa.at[:, x, zl, c], sx + d - 1, dev)
    pass_far("O")
    pass_pair("B")
    pass_near("A")
    gather_x(sa, sx)
    send(sa.at[:, :, zl, c], sa.at[:, :, zl, c], sz, pair)
    pass_own("B")
    lc[2].wait()
    whole("O")

    def coeff(j, _):
        hi, lo = split(owb[j])
        e = eb[...]
        sc[j] = dot(e, hi) + dot(e, lo)
        return 0

    lax.fori_loop(0, 4, coeff, 0)

    pass_far("A")
    arrived(sa.at[:, :, 1 - zl, c], sz)
    send(sa.at[:, :, :, c], sa.at[:, :, :, c], sk, sib)
    arrived(ca.at[:, :, 1 - zl, c], cl)
    send(ca.at[:, :, :, c], ca.at[:, :, :, c], ck, sib)
    pass_pair("C")
    pass_near("B")
    pass_own("C")
    arrived(sa.at[:, :, :, 1 - c], sk)

    def scale(j, _):
        hi, lo = split(sa[j].reshape(128, 256))
        o = ob[...]
        v = sc[j] * (dot(o, hi) + dot(o, lo))
        hi, lo = split(v)
        sh[j] = hi
        sl[j] = lo
        return 0

    lax.fori_loop(0, 4, scale, 0)
    hi, lo = split(sa[4].reshape(128, 256))
    off = dot(ob[...], hi) + dot(ob[...], lo)
    t = (sh[0].astype(F32) + sl[0].astype(F32)) * bias[...] - jnp.minimum(sc[0], 0.0) * off
    rel[...] = t[:, 0:128] + t[:, 128:256]

    rt = take(6)

    def tile(k):
        dy, dz, half = TILES[k]
        block = nid(zh + dz, y + dy)
        cols = pl.ds(pl.multiple_of(block * 512 + half * 256, 256), 256)
        for j in range(4):
            hi, lo = split(wl[:, cols] if j == 0 else wb[j - 1, :, k * 256 : k * 256 + 256])
            whi[j * 256 : (j + 1) * 256, :] = hi
            wlo[j * 256 : (j + 1) * 256, :] = lo
        a = jnp.concatenate([sh[j] for j in range(4)], axis=1)
        b = jnp.concatenate([sl[j] for j in range(4)], axis=1)
        sendb[k] = dot(a, whi[...]) + dot(b, whi[...]) + dot(a, wlo[...])
        if k < 6:
            send(sendb.at[k], recvb.at[k], rt + k, (s, block))

    whole("A")
    for k in range(0, 3):
        tile(k)
    pass_far("B")
    pass_near("C")
    arrived(ca.at[:, :, :, 1 - c], ck)
    for which, dst in ((0, crow), (1, rrow)):
        hi, lo = split(ca[which].reshape(128, 512))
        dst[...] = dot(ob[...], hi) + dot(ob[...], lo)
    pass_far("C")
    whole("B")
    for k in range(3, 6):
        tile(k)
    whole("C")
    tile(6)
    tile(7)

    written = []
    for half, ks in ((0, (0, 1, 2)), (1, (3, 4, 5))):
        cols = slice(half * 256, half * 256 + 256)
        v = sendb[6 + half]
        for k in ks:
            arrived(recvb.at[k], rt + k)
            v = v + recvb[k]
        outb[half] = v
        written.append(pltpu.make_async_copy(outb.at[half], out.at[:, cols], ls.at[half]))
        written[-1].start()
        t = v * crow[:, cols] - jnp.abs(v) * rrow[:, cols]
        rel[...] += t[:, 0:128] + t[:, 128:256]

    mb[n] = jnp.sum(jnp.transpose(rel[...]), axis=0, keepdims=True)
    ms = take(15)
    for d in range(1, 16):
        send(mb.at[n], mb.at[n], ms + d - 1, (s, (n + d) % 16))
    for d in range(1, 16):
        arrived(mb.at[(n + 16 - d) % 16], ms + d - 1)
    marg[...] = jnp.sum(mb[...], axis=0)

    for copy in written:
        copy.wait()
    for copy in started:
        copy.wait_send()


def local(center, radius, weight, bias, out_weight, masks, image_labels, runner_up, spec_image):
    vmem, hbm = pl.BlockSpec(memory_space=pltpu.VMEM), pl.BlockSpec(memory_space=pl.ANY)
    coeffs, margins = pl.pallas_call(
        kernel,
        out_shape=(jax.ShapeDtypeStruct((512, 512), F32), jax.ShapeDtypeStruct((1, 512), F32)),
        in_specs=[hbm, hbm, hbm, vmem, hbm, vmem, vmem, vmem, vmem],
        out_specs=(hbm, vmem),
        scratch_shapes=[
            pltpu.VMEM((256, 8192), F32),
            pltpu.VMEM((3, 256, 2048), F32),
            pltpu.VMEM((4, 1024, 256), F32),
            pltpu.VMEM((4, 4, 2, 8, 512), F32),
            pltpu.VMEM((2, 4, 2, 2, 8, 512), F32),
            pltpu.VMEM((5, 4, 2, 2, 8, 256), F32),
            pltpu.VMEM((4, 512, 256), F32),
            pltpu.VMEM((4, 512, 256), BF16),
            pltpu.VMEM((4, 512, 256), BF16),
            pltpu.VMEM((1024, 256), BF16),
            pltpu.VMEM((1024, 256), BF16),
            pltpu.VMEM((8, 512, 256), F32),
            pltpu.VMEM((6, 512, 256), F32),
            pltpu.VMEM((2, 512, 256), F32),
            pltpu.VMEM((512, 512), F32),
            pltpu.VMEM((512, 512), F32),
            pltpu.VMEM((512, 128), F32),
            pltpu.VMEM((512, 1024), BF16),
            pltpu.VMEM((512, 128), BF16),
            pltpu.VMEM((16, 1, 512), F32),
            pltpu.SemaphoreType.DMA((N_SEND,)),
            pltpu.SemaphoreType.DMA((N_RECV,)),
            pltpu.SemaphoreType.DMA((8,)),
        ],
        compiler_params=pltpu.CompilerParams(
            collective_id=0, has_side_effects=True, vmem_limit_bytes=60 * 1024 * 1024
        ),
        name="bounds",
    )(
        center,
        radius,
        weight,
        bias.reshape(1, 256),
        out_weight,
        masks,
        image_labels.reshape(1, 128),
        runner_up.reshape(1, 512),
        spec_image.reshape(1, 512),
    )
    return coeffs, margins.reshape(512)


def solution(mesh):
    return jax.shard_map(
        local,
        mesh=mesh,
        in_specs=(
            P("spec", "neuron"),
            P("spec", "neuron"),
            P("neuron", None),
            P("neuron"),
            P(None, "neuron"),
            P(None, "neuron"),
            P(),
            P("spec"),
            P("spec"),
        ),
        out_specs=(P("spec", "neuron"), P("spec")),
        check_vma=False,
    )
```

```python
import jax
import jax.numpy as jnp
from jax import lax
from jax.experimental import pallas as pl
from jax.experimental.pallas import tpu as pltpu
from jax.sharding import PartitionSpec as P

MESH = pl.DeviceIdType.MESH
F32, BF16 = jnp.float32, jnp.bfloat16


def split(v):
    hi = v.astype(BF16)
    return hi, (v - hi.astype(F32)).astype(BF16)


def dot(a, b):
    return lax.dot_general(a, b, (((1,), (0,)), ((), ())), preferred_element_type=F32)


def dot_t(a, b):
    return lax.dot_general(a, b, (((1,), (1,)), ((), ())), preferred_element_type=F32)


def sid(x, zl, c):
    return ((x + 4) % 4 * 2 + zl) * 2 + c


def nid(zh, y):
    return (zh + 4) % 4 * 4 + (y + 4) % 4


TILES = ((0, 1, 0), (0, -1, 1), (1, 0, 0), (-1, 0, 0), (1, 0, 1), (-1, 0, 1), (0, 0, 0), (0, 0, 1))
SLOT = (0, 3, 1, 2, 4, 5)
TWICE = "BC"
SPAN = {"A": (0, 2), "B": (2, 4), "C": (4, 6), "D": (6, 8)}
CLASS = ((0, 0), (2, 1), (0, 2), (2, 3))
N_RECV = 69


def kernel(
    center, radius, w, bias, ow, masks, labels, runner, simg, out, marg,
    wl, whl, ahl, wb, owb, cb, ca, sa, sc, sh, sl, whi, wlo, sendb, recvb, outb, crow, rrow, rel, eb, ob, mb,
    bias_v, mask_v, ids_v, ss, rs, ls,
):
    s, n = lax.axis_index("spec"), lax.axis_index("neuron")
    x, zl, c = s // 4, s // 2 % 2, s % 2
    zh, y = n // 4, n % 4

    counter = [0]
    kinds = {
        "o": owb.at[0:3, 0:1000],
        "w": wb,
        "b": cb.at[0:3, 0:2],
        "by": cb,
        "bk": cb.at[0:2],
        "j": sa.at[0:3, 0, 0, 0],
        "sx": sa.at[:, 0:3, 0, 0],
        "s": sa.at[:, 0:3],
        "r": recvb,
        "m": mb.at[0:15],
    }

    def take(k=1):
        counter[0] += k
        assert counter[0] <= N_RECV
        return counter[0] - k

    def send(src, dst, sem, dev, kind):
        pltpu.make_async_remote_copy(
            src_ref=src, dst_ref=dst, send_sem=ss.at[list(kinds).index(kind)], recv_sem=rs.at[sem],
            device_id=dev, device_id_type=MESH,
        ).start()

    def arrived(dst, sem):
        pltpu.make_async_copy(dst, dst, rs.at[sem]).wait()

    lc = [
        pltpu.make_async_copy(center, cb.at[y, zh, 0], ls.at[0]),
        pltpu.make_async_copy(radius, cb.at[y, zh, 1], ls.at[1]),
        pltpu.make_async_copy(ow, owb.at[0, 0:1000], ls.at[2]),
    ]
    for copy in lc:
        copy.start()
    wc = [
        pltpu.make_async_copy(w.at[:, pl.ds(i * 2048, 2048)], wl.at[:, pl.ds(i * 2048, 2048)], ls.at[3 + i])
        for i in range(4)
    ]
    for copy in wc:
        copy.start()
    small = [
        pltpu.make_async_copy(bias, bias_v, ls.at[7]),
        pltpu.make_async_copy(masks.at[pl.ds(pl.multiple_of(8 * s, 8), 8)], mask_v, ls.at[8]),
        pltpu.make_async_copy(labels, ids_v.at[0:1, 0:128], ls.at[9]),
        pltpu.make_async_copy(runner, ids_v.at[1:2], ls.at[10]),
        pltpu.make_async_copy(simg, ids_v.at[2:3], ls.at[11]),
    ]
    for copy in small:
        copy.start()

    right, left, far = (sid(x + 1, zl, c), n), (sid(x - 1, zl, c), n), (sid(x + 2, zl, c), n)
    pair, sib = (sid(x, 1 - zl, c), n), (sid(x, zl, 1 - c), n)
    near = (sid(x, 1 - zl, c), nid(zh + 2 * zl - 1, y + 2))
    across = (sid(x, 1 - zl, c), nid(zh + 2, y))
    peers = [(s, (n + d) % 16) for d in range(1, 16)] + [right, left, far, pair, sib, near, across]
    barrier = pltpu.get_barrier_semaphore()
    for peer in peers:
        pl.semaphore_signal(barrier, inc=1, device_id=peer, device_id_type=MESH)
    pl.semaphore_wait(barrier, len(peers))

    lc[0].wait()
    lc[1].wait()
    cz, cy, cx = take(), take(3), take()
    for d in (1, 2, 3):
        send(cb.at[y, zh], cb.at[y, zh], cz, (s, nid(zh + d, y)), "b")

    j_in, j_out = 3 - 2 * zl, 1 + 2 * zl
    order = (j_in, 2, j_out)
    base = {g: take(11) for g in "OABCD"}
    xl, xr, xf = (x + 3) % 4, (x + 1) % 4, (x + 2) % 4

    def part_o(j, q, start=0, size=120):
        return owb.at[j, pl.ds(pl.multiple_of(480 * c + 120 * q + start, 8), size)]

    def half_o(h):
        start = 480 * c + 120 * x
        first = pl.ds(pl.multiple_of(start + 80 * h, 8), 40)
        second = pl.ds(pl.multiple_of(jnp.where(h == 0, start + 40, 960), 8), 40)
        return first, second

    def fetch_o():
        rows = pl.ds(pl.multiple_of(480 * c + 120 * x, 8), 120)
        send(ow.at[rows], owb.at[j_out, rows], base["O"], near, "o")
        send(ow.at[960:1000], owb.at[j_out, 960:1000], base["O"], near, "o")
        for rows in half_o(1 - zl):
            send(ow.at[rows], owb.at[2, rows], base["O"] + 1, across, "o")

    def ring_o(j):
        send(part_o(j, x), part_o(j, x), base["O"] + 3 + j, right, "o")
        send(part_o(j, x), part_o(j, x), base["O"] + 3 + j, left, "o")

    def pair_o_block():
        arrived(owb.at[j_in, 0:160], base["O"])
        ring_o(j_in)
        send(part_o(j_in, x), part_o(j_in, x), base["O"] + 2, pair, "o")
        send(owb.at[j_in, 960:1000], owb.at[j_in, 960:1000], base["O"] + 2, pair, "o")

    def pair_o_half():
        arrived(owb.at[2, 0:80], base["O"] + 1)
        for rows in half_o(zl):
            send(owb.at[2, rows], owb.at[2, rows], base["O"] + 3, pair, "o")

    def own_o():
        arrived(owb.at[2, 0:80], base["O"] + 3)
        ring_o(2)
        arrived(owb.at[j_out, 0:160], base["O"] + 2)
        ring_o(j_out)

    def near_o(js):
        for j in js:
            arrived(owb.at[j, 0:240], base["O"] + 3 + j)
            send(part_o(j, xl, 0, 64), part_o(j, xl, 0, 64), base["O"] + 6 + j, right, "o")
            send(part_o(j, xr, 64, 56), part_o(j, xr, 64, 56), base["O"] + 6 + j, left, "o")

    def far_o():
        for j in order:
            arrived(part_o(j, xf), base["O"] + 6 + j)
            rows = pl.ds(pl.multiple_of(480 * c, 8), 480)
            send(owb.at[j, rows], owb.at[j, rows], base["O"] + 10, sib, "o")

    def rows_w(start, size):
        return pl.ds(pl.multiple_of(128 * c + start, 16), size)

    def cols_w(g):
        lo, hi = SPAN[g]
        return slice(lo * 256, hi * 256)

    def part_w(g, j, q, start=0, size=32):
        return wb.at[j - 1, rows_w(64 * (q % 2) + 32 * (q // 2) + start, size), cols_w(g)]

    def block_in(g, j):
        return wb.at[j - 1, rows_w(64 * (x % 2), 64), cols_w(g)] if g in TWICE else part_w(g, j, x)

    def half_in(g, h):
        if g in TWICE:
            return wb.at[1, rows_w(64 * (x % 2) + 32 * h, 32), cols_w(g)]
        return part_w(g, 2, x, 16 * h, 16)

    def fetch(g):
        lo, hi = SPAN[g]
        unit = 64 if g in TWICE else 32
        first = 64 * (x % 2) + (0 if g in TWICE else 32 * (x // 2))
        for dev, zd, yd, j, start, size in (
            (near, zh + 2 * zl - 1, y + 2, j_out, 0, unit),
            (across, zh + 2, y, 2, unit // 2 * (1 - zl), unit // 2),
        ):
            rows = rows_w(first + start, size)
            k = lo
            while k < hi:
                dy, dz, half = TILES[k]
                wide = 512 if k == 6 else 256
                cols = pl.ds(pl.multiple_of(nid(zd + dz, yd + dy) * 512 + half * 256, 256), wide)
                sem = base[g] + (0 if size == unit else 1)
                send(w.at[rows, cols], wb.at[j - 1, rows, k * 256 : k * 256 + wide], sem, dev, "w")
                k += wide // 256

    def pair_w(g):
        arrived(block_in(g, j_in), base[g])
        send(block_in(g, j_in), block_in(g, j_in), base[g] + 2, pair, "w")
        arrived(half_in(g, zl), base[g] + 1)
        send(half_in(g, zl), half_in(g, zl), base[g] + 3, pair, "w")

    def ring_w(g, js=order):
        for j in js:
            if j is order[1]:
                arrived(half_in(g, 1 - zl), base[g] + 3)
            elif j is order[2]:
                arrived(block_in(g, j), base[g] + 2)
            send(part_w(g, j, x), part_w(g, j, x), base[g] + 3 + j, right, "w")
            send(part_w(g, j, x), part_w(g, j, x), base[g] + 3 + j, left, "w")

    def core_w(g):
        for j in order:
            arrived(wb.at[j - 1, 0:64, cols_w(g)], base[g] + 3 + j)
            half = wb.at[j - 1, rows_w(0, 128), cols_w(g)]
            send(half, half, base[g] + 10, sib, "w")

    def near_w(g, js=order):
        for j in js:
            arrived(wb.at[j - 1, 0:64, cols_w(g)], base[g] + 3 + j)
            send(part_w(g, j, xl, 0, 16), part_w(g, j, xl, 0, 16), base[g] + 6 + j, right, "w")
            send(part_w(g, j, xr, 16, 16), part_w(g, j, xr, 16, 16), base[g] + 6 + j, left, "w")

    def far_w(g):
        for j in order:
            arrived(part_w(g, j, xf), base[g] + 6 + j)
            half = wb.at[j - 1, rows_w(0, 128), cols_w(g)]
            send(half, half, base[g] + 10, sib, "w")

    def whole_w(g):
        arrived(wb.at[:, 0:128, cols_w(g)], base[g] + 10)

    fetch_o()
    for dev in (right, far, left):
        send(cb.at[y, zh], ca.at[:, x, zl, c], cx, dev, "b")
    for i in range(4):
        wc[i].wait()

        def parts(k, _):
            cols = pl.ds(pl.multiple_of(k * 256, 256), 256)
            v = wl[:, cols]
            whl[0, :, cols], whl[1, :, cols] = split(v)
            ahl[0, :, cols], ahl[1, :, cols] = split(jnp.abs(v))
            return 0

        lax.fori_loop(8 * i, 8 * i + 8, parts, 0)
    arrived(cb.at[0, 0:3], cz)
    for d in (1, 2, 3):
        send(cb.at[y], cb.at[y], cy + d - 1, (s, nid(zh, y + d)), "by")

    for copy in small:
        copy.wait()
    img = jnp.transpose(jnp.broadcast_to(ids_v[2:3], (128, 512)))
    run = jnp.transpose(jnp.broadcast_to(ids_v[1:2], (128, 512)))[:, 0:1]
    picked = img == lax.broadcasted_iota(jnp.int32, (512, 128), 1)
    ob[...] = jnp.where(picked, 1.0, 0.0).astype(BF16)
    label = ids_v[0:1, 0:128].astype(F32)
    lab = jnp.sum(jnp.where(picked, label, 0.0), axis=1, keepdims=True).astype(jnp.int32)
    for k in range(8):
        ids = lax.broadcasted_iota(jnp.int32, (512, 128), 1) + k * 128
        e = jnp.where(ids == lab, 1.0, 0.0) - jnp.where(ids == run, 1.0, 0.0)
        eb[:, k * 128 : (k + 1) * 128] = e.astype(BF16)
    for j in range(4):
        owb[j, 1000:1024, :] = jnp.zeros((24, 256), F32)
    ca[:, x, zl, c] = cb[y, zh]

    def pre_row(yy, carry):
        def body(k, carry):
            pc, pr = carry
            cols = pl.ds(pl.multiple_of((k * 4 + yy) * 512, 512), 512)
            chi, clo = split(cb[yy, k, 0])
            rhi, rlo = split(cb[yy, k, 1])
            cc, rr = jnp.concatenate([chi, clo], axis=0), jnp.concatenate([rhi, rlo], axis=0)
            pc = pc + dot_t(cc, whl[0, :, cols]) + dot_t(cc, whl[1, :, cols])
            pr = pr + dot_t(rr, ahl[0, :, cols]) + dot_t(rr, ahl[1, :, cols])
            return pc, pr

        return lax.fori_loop(0, 4, body, carry, unroll=True)

    zero = jnp.zeros((16, 256), F32)
    carry = pre_row(y, (zero, zero))
    pair_o_block()
    fetch("A")
    pair_o_half()
    def more(d, carry):
        arrived(cb.at[(y + 4 - d) % 4], cy + d - 1)
        return pre_row((y + 4 - d) % 4, carry)

    carry = more(1, carry)
    pair_w("A")
    ring_w("A", order[:1])
    fetch("B")
    own_o()
    carry = more(2, carry)
    carry = more(3, carry)
    pc = carry[0][0:8] + carry[0][8:16] + bias_v[...]
    pr = carry[1][0:8] + carry[1][8:16]
    upper, lower = pc + pr, pc - pr
    slope = jnp.clip(upper / (upper - lower), 0.0, 1.0)
    m = mask_v[...]
    sa[0, x, zl, c] = jnp.where(m == 1, 1.0, jnp.where(m == 2, slope, 0.0))
    sa[4, x, zl, c] = jnp.where(m == 2, slope * lower, 0.0)
    sj = take()
    for j in (1, 2, 3):
        dy, dz = CLASS[j]
        send(sa.at[0, x, zl, c], sa.at[j, x, zl, c], sj, (s, nid(zh - dz, y - dy)), "j")
    fetch("C")
    near_o(order[:2])
    pair_w("B")
    near_o(order[2:])
    arrived(sa.at[0:3, 0, 0, 0], sj)
    sx, sz, sk = take(), take(), take()
    for dev in (right, far, left):
        send(sa.at[:, x, zl, c], sa.at[:, x, zl, c], sx, dev, "sx")
    ring_w("A", order[1:])
    ring_w("B", order[:1])
    far_o()
    arrived(sa.at[:, 0:3, 0, 0], sx)
    send(sa.at[:, :, zl, c], sa.at[:, :, zl, c], sz, pair, "s")
    fetch("D")
    near_w("A")
    pair_w("C")
    ring_w("B", order[1:])
    cl, ck = take(), take()
    arrived(ca.at[:, 0:3, 0, 0], cx)
    send(ca.at[:, :, zl, c], ca.at[:, :, zl, c], cl, pair, "by")
    lc[2].wait()
    arrived(owb.at[0:3, 0:480], base["O"] + 10)

    def coeff(k, _):
        e = eb[...]
        for j in (2 * k, 2 * k + 1):
            hi, lo = split(owb[j])
            sc[j] = dot(e, hi) + dot(e, lo)
        return 0

    lax.fori_loop(0, 2, coeff, 0)

    arrived(sa.at[:, :, 1 - zl, c], sz)
    send(sa.at[:, :, :, c], sa.at[:, :, :, c], sk, sib, "s")
    far_w("A")
    ring_w("C", order[:1])
    pair_w("D")
    arrived(sa.at[:, :, :, 1 - c], sk)

    def scale(k, _):
        o = ob[...]
        for j in (2 * k, 2 * k + 1):
            hi, lo = split(sa[j].reshape(128, 256))
            v = sc[j] * (dot(o, hi) + dot(o, lo))
            hi, lo = split(v)
            sh[j] = hi
            sl[j] = lo
        return 0

    lax.fori_loop(0, 2, scale, 0)
    rt = take(2)

    def prep(k):
        dy, dz, half = TILES[k]
        cols = pl.ds(pl.multiple_of(nid(zh + dz, y + dy) * 512 + half * 256, 256), 256)
        whi[k % 2, 0:256, :] = whl[0, :, cols]
        wlo[k % 2, 0:256, :] = whl[1, :, cols]
        for j in (1, 2, 3):
            hi, lo = split(wb[j - 1, :, k * 256 : k * 256 + 256])
            whi[k % 2, j * 256 : (j + 1) * 256, :] = hi
            wlo[k % 2, j * 256 : (j + 1) * 256, :] = lo

    def mul(k):
        a = jnp.concatenate([sh[j] for j in range(4)], axis=1)
        b = jnp.concatenate([sl[j] for j in range(4)], axis=1)
        for i in (0, 1):
            sendb[k + i] = dot(a, whi[i]) + dot(b, whi[i]) + dot(a, wlo[i])

    def pass_sum(k):
        dy, dz, half = TILES[k]
        send(sendb.at[k], recvb.at[SLOT[k]], rt + half, (s, nid(zh + dz, y + dy)), "r")

    whole_w("A")
    prep(0)
    prep(1)
    mul(0)
    pass_sum(0)
    pass_sum(1)
    core_w("B")
    ring_w("C", order[1:])
    whole_w("B")
    prep(2)
    prep(3)
    mul(2)
    pass_sum(2)
    pass_sum(3)
    ring_w("D")
    arrived(ca.at[:, :, 1 - zl, c], cl)
    send(ca.at[:, :, :, c], ca.at[:, :, :, c], ck, sib, "bk")
    core_w("C")
    whole_w("C")
    prep(4)
    prep(5)
    mul(4)
    pass_sum(4)
    pass_sum(5)
    hi, lo = split(sa[4].reshape(128, 256))
    off = dot(ob[...], hi) + dot(ob[...], lo)
    t = (sh[0].astype(F32) + sl[0].astype(F32)) * bias_v[...] - jnp.minimum(sc[0], 0.0) * off
    rel[...] = t[:, 0:128] + t[:, 128:256]
    near_w("D")
    arrived(ca.at[:, :, :, 1 - c], ck)
    for which, dst in ((0, crow), (1, rrow)):
        hi, lo = split(ca[which].reshape(128, 512))
        dst[...] = dot(ob[...], hi) + dot(ob[...], lo)
    far_w("D")
    whole_w("D")
    prep(6)
    prep(7)
    mul(6)

    written = []
    for half in (0, 1):
        cols = slice(half * 256, half * 256 + 256)
        arrived(recvb.at[0:3], rt + half)
        v = sendb[6 + half] + recvb[3 * half] + recvb[3 * half + 1] + recvb[3 * half + 2]
        outb[half] = v
        written.append(pltpu.make_async_copy(outb.at[half], out.at[:, cols], ls.at[half]))
        written[-1].start()
        t = v * crow[:, cols] - jnp.abs(v) * rrow[:, cols]
        rel[...] += t[:, 0:128] + t[:, 128:256]

    mb[n] = jnp.sum(jnp.transpose(rel[...]), axis=0, keepdims=True)
    ms = take()
    for d in range(1, 16):
        send(mb.at[n], mb.at[n], ms, (s, (n + d) % 16), "m")
    arrived(mb.at[0:15], ms)
    marg[...] = jnp.sum(mb[...], axis=0)

    for copy in written:
        copy.wait()
    for i, all_of_it in enumerate(kinds.values()):
        pltpu.make_async_copy(all_of_it, all_of_it, ss.at[i]).wait()


def finish(coeffs, margins, out, marg, held, row, sems):
    rows = [pl.ds(i * 128, 128) for i in range(4)]
    into = [pltpu.make_async_copy(coeffs.at[r], held.at[r], sems.at[i]) for i, r in enumerate(rows)]
    into.append(pltpu.make_async_copy(margins, row, sems.at[4]))
    back = [pltpu.make_async_copy(held.at[r], out.at[r], sems.at[5 + i]) for i, r in enumerate(rows)]
    back.append(pltpu.make_async_copy(row, marg, sems.at[9]))
    for copy in into:
        copy.start()
    for first, second in zip(into, back):
        first.wait()
        second.start()
    for copy in back:
        copy.wait()


def local(center, radius, weight, bias, out_weight, masks, image_labels, runner_up, spec_image):
    vmem, hbm = pl.BlockSpec(memory_space=pltpu.VMEM), pl.BlockSpec(memory_space=pl.ANY)
    coeffs, margins = pl.pallas_call(
        kernel,
        out_shape=(jax.ShapeDtypeStruct((512, 512), F32), jax.ShapeDtypeStruct((1, 512), F32)),
        in_specs=[hbm] * 9,
        out_specs=(hbm, vmem),
        scratch_shapes=[
            pltpu.VMEM((256, 8192), F32),
            pltpu.VMEM((2, 256, 8192), BF16),
            pltpu.VMEM((2, 256, 8192), BF16),
            pltpu.VMEM((3, 256, 2048), F32),
            pltpu.VMEM((4, 1024, 256), F32),
            pltpu.VMEM((4, 4, 2, 8, 512), F32),
            pltpu.VMEM((2, 4, 2, 2, 8, 512), F32),
            pltpu.VMEM((5, 4, 2, 2, 8, 256), F32),
            pltpu.VMEM((4, 512, 256), F32),
            pltpu.VMEM((4, 512, 256), BF16),
            pltpu.VMEM((4, 512, 256), BF16),
            pltpu.VMEM((2, 1024, 256), BF16),
            pltpu.VMEM((2, 1024, 256), BF16),
            pltpu.VMEM((8, 512, 256), F32),
            pltpu.VMEM((6, 512, 256), F32),
            pltpu.VMEM((2, 512, 256), F32),
            pltpu.VMEM((512, 512), F32),
            pltpu.VMEM((512, 512), F32),
            pltpu.VMEM((512, 128), F32),
            pltpu.VMEM((512, 1024), BF16),
            pltpu.VMEM((512, 128), BF16),
            pltpu.VMEM((16, 1, 512), F32),
            pltpu.VMEM((1, 256), F32),
            pltpu.VMEM((8, 256), jnp.int32),
            pltpu.VMEM((3, 512), jnp.int32),
            pltpu.SemaphoreType.DMA((10,)),
            pltpu.SemaphoreType.DMA((N_RECV,)),
            pltpu.SemaphoreType.DMA((12,)),
        ],
        compiler_params=pltpu.CompilerParams(
            collective_id=0, has_side_effects=True, vmem_limit_bytes=60 * 1024 * 1024
        ),
        name="bounds",
    )(
        center,
        radius,
        weight,
        bias.reshape(1, 256),
        out_weight,
        masks,
        image_labels.reshape(1, 128),
        runner_up.reshape(1, 512),
        spec_image.reshape(1, 512),
    )
    coeffs, margins = pl.pallas_call(
        finish,
        out_shape=(jax.ShapeDtypeStruct((512, 512), F32), jax.ShapeDtypeStruct((1, 512), F32)),
        in_specs=[hbm, hbm],
        out_specs=(hbm, hbm),
        scratch_shapes=[
            pltpu.VMEM((512, 512), F32),
            pltpu.VMEM((1, 512), F32),
            pltpu.SemaphoreType.DMA((10,)),
        ],
        name="finish",
    )(coeffs, margins)
    return coeffs, margins.reshape(512)


def solution(mesh):
    return jax.shard_map(
        local,
        mesh=mesh,
        in_specs=(
            P("spec", "neuron"),
            P("spec", "neuron"),
            P("neuron", None),
            P("neuron"),
            P(None, "neuron"),
            P(None, "neuron"),
            P(),
            P("spec"),
            P("spec"),
        ),
        out_specs=(P("spec", "neuron"), P("spec")),
        check_vma=False,
    )
```

```python
import jax
import jax.numpy as jnp
from jax import lax
from jax.experimental import pallas as pl
from jax.experimental.pallas import tpu as pltpu
from jax.sharding import PartitionSpec as P

MESH = pl.DeviceIdType.MESH
F32, BF16 = jnp.float32, jnp.bfloat16


def split(v):
    hi = v.astype(BF16)
    return hi, (v - hi.astype(F32)).astype(BF16)


def dot(a, b):
    return lax.dot_general(a, b, (((1,), (0,)), ((), ())), preferred_element_type=F32)


def dot_t(a, b):
    return lax.dot_general(a, b, (((1,), (1,)), ((), ())), preferred_element_type=F32)


def sid(x, zl, c):
    return ((x + 4) % 4 * 2 + zl) * 2 + c


def nid(zh, y):
    return (zh + 4) % 4 * 4 + (y + 4) % 4


TILES = ((0, 1, 0), (0, -1, 1), (1, 0, 0), (-1, 0, 0), (1, 0, 1), (-1, 0, 1), (0, 0, 0), (0, 0, 1))
SLOT = (0, 3, 1, 2, 4, 5)
TWICE = "AB"
SPAN = {"A": (0, 2), "B": (2, 4), "C": (4, 6), "D": (6, 8)}
CLASS = ((0, 0), (2, 1), (0, 2), (2, 3))
N_RECV = 73


def kernel(
    center, radius, w, bias, ow, masks, labels, runner, simg, out, marg,
    wl, whl, ahl, wb, owb, cb, ca, sa, sc, sh, sl, whi, wlo, sendb, recvb, outb, crow, rrow, rel, eb, ob, mb,
    bias_v, mask_v, ids_v, ss, rs, ls,
):
    s, n = lax.axis_index("spec"), lax.axis_index("neuron")
    x, zl, c = s // 4, s // 2 % 2, s % 2
    zh, y = n // 4, n % 4

    counter = [0]
    kinds = {
        "o": owb.at[0:3, 0:1000],
        "w": wb,
        "b": cb.at[0:3, 0:2],
        "by": cb,
        "bk": cb.at[0:2],
        "j": sa.at[0:3, 0, 0, 0],
        "sx": owb.at[0, 0:280],
        "s": sa.at[:, 0:2],
        "r": recvb,
        "m": mb.at[0:15],
    }

    def take(k=1):
        counter[0] += k
        assert counter[0] <= N_RECV
        return counter[0] - k

    def send(src, dst, sem, dev, kind):
        pltpu.make_async_remote_copy(
            src_ref=src, dst_ref=dst, send_sem=ss.at[list(kinds).index(kind)], recv_sem=rs.at[sem],
            device_id=dev, device_id_type=MESH,
        ).start()

    def arrived(dst, sem):
        pltpu.make_async_copy(dst, dst, rs.at[sem]).wait()

    lc = [
        pltpu.make_async_copy(center, cb.at[y, zh, 0], ls.at[0]),
        pltpu.make_async_copy(radius, cb.at[y, zh, 1], ls.at[1]),
        pltpu.make_async_copy(ow, owb.at[0, 0:1000], ls.at[2]),
    ]
    small = [
        pltpu.make_async_copy(bias, bias_v, ls.at[7]),
        pltpu.make_async_copy(masks.at[pl.ds(pl.multiple_of(8 * s, 8), 8)], mask_v, ls.at[8]),
        pltpu.make_async_copy(labels, ids_v.at[0:1, 0:128], ls.at[9]),
        pltpu.make_async_copy(runner, ids_v.at[1:2], ls.at[10]),
        pltpu.make_async_copy(simg, ids_v.at[2:3], ls.at[11]),
    ]
    wc = [
        pltpu.make_async_copy(w.at[:, pl.ds(i * 2048, 2048)], wl.at[:, pl.ds(i * 2048, 2048)], ls.at[3 + i])
        for i in range(4)
    ]
    for copy in lc[:2] + small:
        copy.start()

    right, left, far = (sid(x + 1, zl, c), n), (sid(x - 1, zl, c), n), (sid(x + 2, zl, c), n)
    pair, sib = (sid(x, 1 - zl, c), n), (sid(x, zl, 1 - c), n)
    near = (sid(x, 1 - zl, c), nid(zh + 2 * zl - 1, y + 2))
    across = (sid(x, 1 - zl, c), nid(zh + 2, y))
    others = [(sid(x + d, zl + e - 2 * zl * e, c), n) for d in range(4) for e in (0, 1) if d or e]
    peers = [(s, (n + d) % 16) for d in range(1, 16)] + others + [sib, near, across]
    barrier = pltpu.get_barrier_semaphore()
    for peer in peers:
        pl.semaphore_signal(barrier, inc=1, device_id=peer, device_id_type=MESH)
    for copy in wc + lc[2:]:
        copy.start()
    for copy in small:
        copy.wait()
    img = jnp.transpose(jnp.broadcast_to(ids_v[2:3], (128, 512)))
    run = jnp.transpose(jnp.broadcast_to(ids_v[1:2], (128, 512)))[:, 0:1]
    picked = img == lax.broadcasted_iota(jnp.int32, (512, 128), 1)
    ob[...] = jnp.where(picked, 1.0, 0.0).astype(BF16)
    label = ids_v[0:1, 0:128].astype(F32)
    lab = jnp.sum(jnp.where(picked, label, 0.0), axis=1, keepdims=True).astype(jnp.int32)
    for k in range(8):
        ids = lax.broadcasted_iota(jnp.int32, (512, 128), 1) + k * 128
        e = jnp.where(ids == lab, 1.0, 0.0) - jnp.where(ids == run, 1.0, 0.0)
        eb[:, k * 128 : (k + 1) * 128] = e.astype(BF16)
    for j in range(4):
        owb[j, 1000:1024, :] = jnp.zeros((24, 256), F32)
    pl.semaphore_wait(barrier, len(peers))

    lc[0].wait()
    lc[1].wait()
    cz, cy, cx = take(), take(3), take()
    for d in (1, 2, 3):
        send(cb.at[y, zh], cb.at[y, zh], cz, (s, nid(zh + d, y)), "b")

    j_in, j_out = 3 - 2 * zl, 1 + 2 * zl
    order = (j_in, j_out, 2)
    base = {g: take(8 if g in TWICE else 11) for g in "OPABCD"}
    xl, xr, xf = (x + 3) % 4, (x + 1) % 4, (x + 2) % 4

    def part_o(g, j, q, start=0, size=120):
        rows = pl.ds(pl.multiple_of(480 * c + 120 * q + start, 8), size)
        return owb.at[j, rows, cols_o(g)]

    def cols_o(g):
        return slice(0, 128) if g == "O" else slice(128, 256)

    def half_o(h):
        start = 480 * c + 120 * x
        first = pl.ds(pl.multiple_of(start + 80 * h, 8), 40)
        second = pl.ds(pl.multiple_of(jnp.where(h == 0, start + 40, 960), 8), 40)
        return first, second

    def fetch_o(g):
        for rows in (pl.ds(pl.multiple_of(480 * c + 120 * x, 8), 120), slice(960, 1000)):
            send(ow.at[rows, cols_o(g)], owb.at[j_out, rows, cols_o(g)], base[g], near, "o")

    def fetch_o_half(g):
        for rows in half_o(1 - zl):
            send(ow.at[rows, cols_o(g)], owb.at[2, rows, cols_o(g)], base[g] + 1, across, "o")

    def ring_o(g, j):
        send(part_o(g, j, x), part_o(g, j, x), base[g] + 3 + j, right, "o")
        send(part_o(g, j, x), part_o(g, j, x), base[g] + 3 + j, left, "o")

    def pair_o_block(g):
        arrived(owb.at[j_in, 0:160, cols_o(g)], base[g])
        ring_o(g, j_in)
        send(part_o(g, j_in, x), part_o(g, j_in, x), base[g] + 2, pair, "o")
        rest = owb.at[j_in, 960:1000, cols_o(g)]
        send(rest, rest, base[g] + 2, pair, "o")

    def pair_o_half(g):
        arrived(owb.at[2, 0:80, cols_o(g)], base[g] + 1)
        for rows in half_o(zl):
            send(owb.at[2, rows, cols_o(g)], owb.at[2, rows, cols_o(g)], base[g] + 3, pair, "o")

    def own_o_out(g):
        arrived(owb.at[j_out, 0:160, cols_o(g)], base[g] + 2)
        ring_o(g, j_out)

    def own_o_half(g):
        arrived(owb.at[2, 0:80, cols_o(g)], base[g] + 3)
        ring_o(g, 2)

    def near_o(g, js=order):
        for j in js:
            arrived(owb.at[j, 0:240, cols_o(g)], base[g] + 3 + j)
            send(part_o(g, j, xl, 0, 64), part_o(g, j, xl, 0, 64), base[g] + 6 + j, right, "o")
            send(part_o(g, j, xr, 64, 56), part_o(g, j, xr, 64, 56), base[g] + 6 + j, left, "o")

    def far_o(g):
        for j in order:
            arrived(part_o(g, j, xf), base[g] + 6 + j)
            rows = pl.ds(pl.multiple_of(480 * c, 8), 480)
            send(owb.at[j, rows, cols_o(g)], owb.at[j, rows, cols_o(g)], base[g] + 10, sib, "o")

    def rows_w(start, size):
        return pl.ds(pl.multiple_of(128 * c + start, 16), size)

    def cols_w(g):
        lo, hi = SPAN[g]
        return slice(lo * 256, hi * 256)

    def part_w(g, j, q, start=0, size=32):
        return wb.at[j - 1, rows_w(64 * (q % 2) + 32 * (q // 2) + start, size), cols_w(g)]

    def block_in(g, j):
        return wb.at[j - 1, rows_w(64 * (x % 2), 64), cols_w(g)] if g in TWICE else part_w(g, j, x)

    def half_in(g, h):
        if g in TWICE:
            return wb.at[1, rows_w(64 * (x % 2) + 32 * h, 32), cols_w(g)]
        return part_w(g, 2, x, 16 * h, 16)

    def fetch(g):
        lo, hi = SPAN[g]
        unit = 64 if g in TWICE else 32
        first = 64 * (x % 2) + (0 if g in TWICE else 32 * (x // 2))
        for dev, zd, yd, j, start, size in (
            (near, zh + 2 * zl - 1, y + 2, j_out, 0, unit),
            (across, zh + 2, y, 2, unit // 2 * (1 - zl), unit // 2),
        ):
            rows = rows_w(first + start, size)
            k = lo
            while k < hi:
                dy, dz, half = TILES[k]
                wide = 512 if k == 6 else 256
                cols = pl.ds(pl.multiple_of(nid(zd + dz, yd + dy) * 512 + half * 256, 256), wide)
                sem = base[g] + (0 if size == unit else 1)
                send(w.at[rows, cols], wb.at[j - 1, rows, k * 256 : k * 256 + wide], sem, dev, "w")
                k += wide // 256

    def pair_w(g):
        arrived(block_in(g, j_in), base[g])
        send(block_in(g, j_in), block_in(g, j_in), base[g] + 2, pair, "w")
        arrived(half_in(g, zl), base[g] + 1)
        send(half_in(g, zl), half_in(g, zl), base[g] + 3, pair, "w")

    def ring_w(g, js=order):
        for j in js:
            if j is order[1]:
                arrived(block_in(g, j), base[g] + 2)
            elif j is order[2]:
                arrived(half_in(g, 1 - zl), base[g] + 3)
            send(part_w(g, j, x), part_w(g, j, x), base[g] + 3 + j, right, "w")
            send(part_w(g, j, x), part_w(g, j, x), base[g] + 3 + j, left, "w")

    def core_w(g):
        for j in order:
            arrived(wb.at[j - 1, 0:64, cols_w(g)], base[g] + 3 + j)
            half = wb.at[j - 1, rows_w(0, 128), cols_w(g)]
            send(half, half, base[g] + 7, sib, "w")

    def near_w(g, js=order):
        for j in js:
            arrived(wb.at[j - 1, 0:64, cols_w(g)], base[g] + 3 + j)
            send(part_w(g, j, xl, 0, 16), part_w(g, j, xl, 0, 16), base[g] + 6 + j, right, "w")
            send(part_w(g, j, xr, 16, 16), part_w(g, j, xr, 16, 16), base[g] + 6 + j, left, "w")

    def far_w(g):
        for j in order:
            arrived(part_w(g, j, xf), base[g] + 6 + j)
            half = wb.at[j - 1, rows_w(0, 128), cols_w(g)]
            send(half, half, base[g] + 10, sib, "w")

    def whole_w(g):
        arrived(wb.at[:, 0:128, cols_w(g)], base[g] + (7 if g in TWICE else 10))

    for g in "OP":
        fetch_o(g)
    for g in "OP":
        fetch_o_half(g)
    for dev in (right, far, left):
        send(cb.at[y, zh], ca.at[:, x, zl, c], cx, dev, "b")
    arrived(cb.at[0, 0:3], cz)
    for d in (1, 2, 3):
        send(cb.at[y], cb.at[y], cy + d - 1, (s, nid(zh, y + d)), "by")

    for i in range(4):
        wc[i].wait()

        def parts(k, _):
            cols = pl.ds(pl.multiple_of(k * 256, 256), 256)
            v = wl[:, cols]
            whl[0, :, cols], whl[1, :, cols] = split(v)
            ahl[0, :, cols], ahl[1, :, cols] = split(jnp.abs(v))
            return 0

        lax.fori_loop(8 * i, 8 * i + 8, parts, 0)
    ca[:, x, zl, c] = cb[y, zh]

    def pre_row(yy, carry):
        def body(k, carry):
            pc, pr = carry
            cols = pl.ds(pl.multiple_of((k * 4 + yy) * 512, 512), 512)
            chi, clo = split(cb[yy, k, 0])
            rhi, rlo = split(cb[yy, k, 1])
            cc, rr = jnp.concatenate([chi, clo], axis=0), jnp.concatenate([rhi, rlo], axis=0)
            pc = pc + dot_t(cc, whl[0, :, cols]) + dot_t(cc, whl[1, :, cols])
            pr = pr + dot_t(rr, ahl[0, :, cols]) + dot_t(rr, ahl[1, :, cols])
            return pc, pr

        return lax.fori_loop(0, 4, body, carry, unroll=True)

    zero = jnp.zeros((16, 256), F32)
    carry = pre_row(y, (zero, zero))
    pair_o_block("O")
    pair_o_block("P")
    fetch("A")
    pair_o_half("O")
    pair_o_half("P")
    def more(d, carry):
        arrived(cb.at[(y + 4 - d) % 4], cy + d - 1)
        return pre_row((y + 4 - d) % 4, carry)

    carry = more(1, carry)
    own_o_out("O")
    own_o_out("P")
    pair_w("A")
    ring_w("A", order[:1])
    fetch("B")
    own_o_half("O")
    own_o_half("P")
    carry = more(2, carry)
    carry = more(3, carry)
    pc = carry[0][0:8] + carry[0][8:16] + bias_v[...]
    pr = carry[1][0:8] + carry[1][8:16]
    upper, lower = pc + pr, pc - pr
    slope = jnp.clip(upper / (upper - lower), 0.0, 1.0)
    m = mask_v[...]
    sa[0, x, zl, c] = jnp.where(m == 1, 1.0, jnp.where(m == 2, slope, 0.0))
    sa[4, x, zl, c] = jnp.where(m == 2, slope * lower, 0.0)
    sj = take()
    for j in (1, 2, 3):
        dy, dz = CLASS[j]
        send(sa.at[0, x, zl, c], sa.at[j, x, zl, c], sj, (s, nid(zh - dz, y - dy)), "j")
    near_o("O", order[:2])
    near_o("P", order[:2])
    near_o("O", order[2:])
    near_o("P", order[2:])
    ring_w("A", order[1:])
    pair_w("B")
    fetch("C")
    fetch("D")
    arrived(sa.at[0:3, 0, 0, 0], sj)
    sx, sk = take(), take()
    for dev in others:
        send(sa.at[:, x, zl, c], sa.at[:, x, zl, c], sx, dev, "sx")
    cl, ck = take(), take()
    arrived(ca.at[:, 0:3, 0, 0], cx)
    send(ca.at[:, :, zl, c], ca.at[:, :, zl, c], cl, pair, "by")
    far_o("O")
    far_o("P")
    ring_w("B", order[:1])
    ring_w("B", order[1:])
    lc[2].wait()
    for g in "OP":
        arrived(owb.at[0:3, 0:480, cols_o(g)], base[g] + 10)

    def coeff(k, _):
        e = eb[...]
        for j in (2 * k, 2 * k + 1):
            hi, lo = split(owb[j])
            sc[j] = dot(e, hi) + dot(e, lo)
        return 0

    lax.fori_loop(0, 2, coeff, 0)

    arrived(owb.at[0, 0:280], sx)
    send(sa.at[:, :, :, c], sa.at[:, :, :, c], sk, sib, "s")
    core_w("A")
    core_w("B")
    pair_w("C")
    pair_w("D")
    ring_w("C", order[:1])
    arrived(sa.at[:, :, :, 1 - c], sk)

    def scale(k, _):
        o = ob[...]
        for j in (2 * k, 2 * k + 1):
            hi, lo = split(sa[j].reshape(128, 256))
            v = sc[j] * (dot(o, hi) + dot(o, lo))
            hi, lo = split(v)
            sh[j] = hi
            sl[j] = lo
        return 0

    lax.fori_loop(0, 2, scale, 0)
    rt = take(2)

    def prep(k):
        dy, dz, half = TILES[k]
        cols = pl.ds(pl.multiple_of(nid(zh + dz, y + dy) * 512 + half * 256, 256), 256)
        whi[k % 2, 0:256, :] = whl[0, :, cols]
        wlo[k % 2, 0:256, :] = whl[1, :, cols]
        for j in (1, 2, 3):
            hi, lo = split(wb[j - 1, :, k * 256 : k * 256 + 256])
            whi[k % 2, j * 256 : (j + 1) * 256, :] = hi
            wlo[k % 2, j * 256 : (j + 1) * 256, :] = lo

    def mul(k):
        a = jnp.concatenate([sh[j] for j in range(4)], axis=1)
        b = jnp.concatenate([sl[j] for j in range(4)], axis=1)
        for i in (0, 1):
            sendb[k + i] = dot(a, whi[i]) + dot(b, whi[i]) + dot(a, wlo[i])

    def pass_sum(k):
        dy, dz, half = TILES[k]
        send(sendb.at[k], recvb.at[SLOT[k]], rt + half, (s, nid(zh + dz, y + dy)), "r")

    whole_w("A")
    prep(0)
    prep(1)
    mul(0)
    pass_sum(0)
    pass_sum(1)
    ring_w("C", order[1:])
    whole_w("B")
    prep(2)
    prep(3)
    mul(2)
    pass_sum(2)
    pass_sum(3)
    near_w("C")
    arrived(ca.at[:, :, 1 - zl, c], cl)
    send(ca.at[:, :, :, c], ca.at[:, :, :, c], ck, sib, "bk")
    ring_w("D")
    far_w("C")
    whole_w("C")
    prep(4)
    prep(5)
    mul(4)
    pass_sum(4)
    pass_sum(5)
    hi, lo = split(sa[4].reshape(128, 256))
    off = dot(ob[...], hi) + dot(ob[...], lo)
    t = (sh[0].astype(F32) + sl[0].astype(F32)) * bias_v[...] - jnp.minimum(sc[0], 0.0) * off
    rel[...] = t[:, 0:128] + t[:, 128:256]
    near_w("D")
    arrived(ca.at[:, :, :, 1 - c], ck)
    for which, dst in ((0, crow), (1, rrow)):
        hi, lo = split(ca[which].reshape(128, 512))
        dst[...] = dot(ob[...], hi) + dot(ob[...], lo)
    far_w("D")
    whole_w("D")
    prep(6)
    prep(7)
    mul(6)

    written = []
    for half in (0, 1):
        cols = slice(half * 256, half * 256 + 256)
        arrived(recvb.at[0:3], rt + half)
        v = sendb[6 + half] + recvb[3 * half] + recvb[3 * half + 1] + recvb[3 * half + 2]
        outb[half] = v
        written.append(pltpu.make_async_copy(outb.at[half], out.at[:, cols], ls.at[half]))
        written[-1].start()
        t = v * crow[:, cols] - jnp.abs(v) * rrow[:, cols]
        rel[...] += t[:, 0:128] + t[:, 128:256]

    mb[n] = jnp.sum(jnp.transpose(rel[...]), axis=0, keepdims=True)
    ms = take()
    for d in range(1, 16):
        send(mb.at[n], mb.at[n], ms, (s, (n + d) % 16), "m")
    arrived(mb.at[0:15], ms)
    marg[...] = jnp.sum(mb[...], axis=0)

    for copy in written:
        copy.wait()
    for i, all_of_it in enumerate(kinds.values()):
        pltpu.make_async_copy(all_of_it, all_of_it, ss.at[i]).wait()


def finish(coeffs, margins, out, marg, held, row, sems):
    rows = [pl.ds(i * 128, 128) for i in range(4)]
    into = [pltpu.make_async_copy(coeffs.at[r], held.at[r], sems.at[i]) for i, r in enumerate(rows)]
    into.append(pltpu.make_async_copy(margins, row, sems.at[4]))
    back = [pltpu.make_async_copy(held.at[r], out.at[r], sems.at[5 + i]) for i, r in enumerate(rows)]
    back.append(pltpu.make_async_copy(row, marg, sems.at[9]))
    for copy in into:
        copy.start()
    for first, second in zip(into, back):
        first.wait()
        second.start()
    for copy in back:
        copy.wait()


def local(center, radius, weight, bias, out_weight, masks, image_labels, runner_up, spec_image):
    vmem, hbm = pl.BlockSpec(memory_space=pltpu.VMEM), pl.BlockSpec(memory_space=pl.ANY)
    coeffs, margins = pl.pallas_call(
        kernel,
        out_shape=(jax.ShapeDtypeStruct((512, 512), F32), jax.ShapeDtypeStruct((1, 512), F32)),
        in_specs=[hbm] * 9,
        out_specs=(hbm, vmem),
        scratch_shapes=[
            pltpu.VMEM((256, 8192), F32),
            pltpu.VMEM((2, 256, 8192), BF16),
            pltpu.VMEM((2, 256, 8192), BF16),
            pltpu.VMEM((3, 256, 2048), F32),
            pltpu.VMEM((4, 1024, 256), F32),
            pltpu.VMEM((4, 4, 2, 8, 512), F32),
            pltpu.VMEM((2, 4, 2, 2, 8, 512), F32),
            pltpu.VMEM((5, 4, 2, 2, 8, 256), F32),
            pltpu.VMEM((4, 512, 256), F32),
            pltpu.VMEM((4, 512, 256), BF16),
            pltpu.VMEM((4, 512, 256), BF16),
            pltpu.VMEM((2, 1024, 256), BF16),
            pltpu.VMEM((2, 1024, 256), BF16),
            pltpu.VMEM((8, 512, 256), F32),
            pltpu.VMEM((6, 512, 256), F32),
            pltpu.VMEM((2, 512, 256), F32),
            pltpu.VMEM((512, 512), F32),
            pltpu.VMEM((512, 512), F32),
            pltpu.VMEM((512, 128), F32),
            pltpu.VMEM((512, 1024), BF16),
            pltpu.VMEM((512, 128), BF16),
            pltpu.VMEM((16, 1, 512), F32),
            pltpu.VMEM((1, 256), F32),
            pltpu.VMEM((8, 256), jnp.int32),
            pltpu.VMEM((3, 512), jnp.int32),
            pltpu.SemaphoreType.DMA((10,)),
            pltpu.SemaphoreType.DMA((N_RECV,)),
            pltpu.SemaphoreType.DMA((12,)),
        ],
        compiler_params=pltpu.CompilerParams(
            collective_id=0, has_side_effects=True, vmem_limit_bytes=60 * 1024 * 1024
        ),
        name="bounds",
    )(
        center,
        radius,
        weight,
        bias.reshape(1, 256),
        out_weight,
        masks,
        image_labels.reshape(1, 128),
        runner_up.reshape(1, 512),
        spec_image.reshape(1, 512),
    )
    coeffs, margins = pl.pallas_call(
        finish,
        out_shape=(jax.ShapeDtypeStruct((512, 512), F32), jax.ShapeDtypeStruct((1, 512), F32)),
        in_specs=[hbm, hbm],
        out_specs=(hbm, hbm),
        scratch_shapes=[
            pltpu.VMEM((512, 512), F32),
            pltpu.VMEM((1, 512), F32),
            pltpu.SemaphoreType.DMA((10,)),
        ],
        name="finish",
    )(coeffs, margins)
    return coeffs, margins.reshape(512)


def solution(mesh):
    return jax.shard_map(
        local,
        mesh=mesh,
        in_specs=(
            P("spec", "neuron"),
            P("spec", "neuron"),
            P("neuron", None),
            P("neuron"),
            P(None, "neuron"),
            P(None, "neuron"),
            P(),
            P("spec"),
            P("spec"),
        ),
        out_specs=(P("spec", "neuron"), P("spec")),
        check_vma=False,
    )
```

```python
import jax
import jax.numpy as jnp
from jax import lax
from jax.experimental import pallas as pl
from jax.experimental.pallas import tpu as pltpu
from jax.sharding import PartitionSpec as P

MESH = pl.DeviceIdType.MESH
F32, BF16 = jnp.float32, jnp.bfloat16


def split(v):
    hi = v.astype(BF16)
    return hi, (v - hi.astype(F32)).astype(BF16)


def dot(a, b):
    return lax.dot_general(a, b, (((1,), (0,)), ((), ())), preferred_element_type=F32)


def dot_t(a, b):
    return lax.dot_general(a, b, (((1,), (1,)), ((), ())), preferred_element_type=F32)


def sid(x, zl, c):
    return ((x + 4) % 4 * 2 + zl) * 2 + c


def nid(zh, y):
    return (zh + 4) % 4 * 4 + (y + 4) % 4


TILES = ((1, 0, 0), (-1, 0, 0), (0, 1, 0), (0, -1, 1), (1, 0, 1), (-1, 0, 1), (0, 0, 0), (0, 0, 1))
SLOT = (0, 1, 2, 3, 4, 5)
TWICE = "AB"
SPAN = {"A": (0, 2), "B": (2, 4), "C": (4, 6), "D": (6, 8)}
CLASS = ((0, 0), (2, 1), (0, 2), (2, 3))
N_RECV = 73


def kernel(
    center, radius, w, bias, ow, masks, labels, runner, simg, out, marg,
    wl, whl, ahl, wb, owb, cb, ca, sa, sc, sh, sl, whi, wlo, sendb, recvb, outb, crow, rrow, rel, eb, ob, mb,
    bias_v, mask_v, ids_v, ss, rs, ls,
):
    s, n = lax.axis_index("spec"), lax.axis_index("neuron")
    x, zl, c = s // 4, s // 2 % 2, s % 2
    zh, y = n // 4, n % 4

    counter = [0]
    kinds = {
        "o": owb.at[0:3, 0:1000],
        "w": wb,
        "b": cb.at[0:3, 0:2],
        "by": cb,
        "bk": cb.at[0:2],
        "j": sa.at[0:3, 0, 0, 0],
        "sx": owb.at[0, 0:280],
        "s": sa.at[:, 0:2],
        "r": recvb,
        "m": mb.at[0:15],
    }

    def take(k=1):
        counter[0] += k
        assert counter[0] <= N_RECV
        return counter[0] - k

    def send(src, dst, sem, dev, kind):
        pltpu.make_async_remote_copy(
            src_ref=src, dst_ref=dst, send_sem=ss.at[list(kinds).index(kind)], recv_sem=rs.at[sem],
            device_id=dev, device_id_type=MESH,
        ).start()

    def arrived(dst, sem):
        pltpu.make_async_copy(dst, dst, rs.at[sem]).wait()

    lc = [
        pltpu.make_async_copy(center, cb.at[y, zh, 0], ls.at[0]),
        pltpu.make_async_copy(radius, cb.at[y, zh, 1], ls.at[1]),
        pltpu.make_async_copy(ow, owb.at[0, 0:1000], ls.at[2]),
    ]
    small = [
        pltpu.make_async_copy(bias, bias_v, ls.at[7]),
        pltpu.make_async_copy(masks.at[pl.ds(pl.multiple_of(8 * s, 8), 8)], mask_v, ls.at[8]),
        pltpu.make_async_copy(labels, ids_v.at[0:1, 0:128], ls.at[9]),
        pltpu.make_async_copy(runner, ids_v.at[1:2], ls.at[10]),
        pltpu.make_async_copy(simg, ids_v.at[2:3], ls.at[11]),
    ]
    wc = [
        pltpu.make_async_copy(w.at[:, pl.ds(i * 2048, 2048)], wl.at[:, pl.ds(i * 2048, 2048)], ls.at[3 + i])
        for i in range(4)
    ]
    for copy in lc[:2] + small:
        copy.start()

    right, left, far = (sid(x + 1, zl, c), n), (sid(x - 1, zl, c), n), (sid(x + 2, zl, c), n)
    pair, sib = (sid(x, 1 - zl, c), n), (sid(x, zl, 1 - c), n)
    near = (sid(x, 1 - zl, c), nid(zh + 2 * zl - 1, y + 2))
    across = (sid(x, 1 - zl, c), nid(zh + 2, y))
    others = [(sid(x + d, zl + e - 2 * zl * e, c), n) for d in range(4) for e in (0, 1) if d or e]
    peers = [(s, (n + d) % 16) for d in range(1, 16)] + others + [sib, near, across]
    barrier = pltpu.get_barrier_semaphore()
    for peer in peers:
        pl.semaphore_signal(barrier, inc=1, device_id=peer, device_id_type=MESH)
    for copy in wc + lc[2:]:
        copy.start()
    for copy in small:
        copy.wait()
    img = jnp.transpose(jnp.broadcast_to(ids_v[2:3], (128, 512)))
    run = jnp.transpose(jnp.broadcast_to(ids_v[1:2], (128, 512)))[:, 0:1]
    picked = img == lax.broadcasted_iota(jnp.int32, (512, 128), 1)
    ob[...] = jnp.where(picked, 1.0, 0.0).astype(BF16)
    label = ids_v[0:1, 0:128].astype(F32)
    lab = jnp.sum(jnp.where(picked, label, 0.0), axis=1, keepdims=True).astype(jnp.int32)
    for k in range(8):
        ids = lax.broadcasted_iota(jnp.int32, (512, 128), 1) + k * 128
        e = jnp.where(ids == lab, 1.0, 0.0) - jnp.where(ids == run, 1.0, 0.0)
        eb[:, k * 128 : (k + 1) * 128] = e.astype(BF16)
    for j in range(4):
        owb[j, 1000:1024, :] = jnp.zeros((24, 256), F32)
    pl.semaphore_wait(barrier, len(peers))

    lc[0].wait()
    lc[1].wait()
    cz, cy, cx = take(), take(3), take()
    for d in (1, 2, 3):
        send(cb.at[y, zh], cb.at[y, zh], cz, (s, nid(zh + d, y)), "b")

    j_in, j_out = 3 - 2 * zl, 1 + 2 * zl
    order = (j_in, j_out, 2)
    base = {g: take(8 if g in TWICE else 11) for g in "OPABCD"}
    xl, xr, xf = (x + 3) % 4, (x + 1) % 4, (x + 2) % 4

    def part_o(g, j, q, start=0, size=120):
        rows = pl.ds(pl.multiple_of(480 * c + 120 * q + start, 8), size)
        return owb.at[j, rows, cols_o(g)]

    def cols_o(g):
        return slice(0, 128) if g == "O" else slice(128, 256)

    def half_o(h):
        start = 480 * c + 120 * x
        first = pl.ds(pl.multiple_of(start + 80 * h, 8), 40)
        second = pl.ds(pl.multiple_of(jnp.where(h == 0, start + 40, 960), 8), 40)
        return first, second

    def fetch_o(g):
        for rows in (pl.ds(pl.multiple_of(480 * c + 120 * x, 8), 120), slice(960, 1000)):
            send(ow.at[rows, cols_o(g)], owb.at[j_out, rows, cols_o(g)], base[g], near, "o")

    def fetch_o_half(g):
        for rows in half_o(1 - zl):
            send(ow.at[rows, cols_o(g)], owb.at[2, rows, cols_o(g)], base[g] + 1, across, "o")

    def ring_o(g, j):
        send(part_o(g, j, x), part_o(g, j, x), base[g] + 3 + j, right, "o")
        send(part_o(g, j, x), part_o(g, j, x), base[g] + 3 + j, left, "o")

    def pair_o_block(g):
        arrived(owb.at[j_in, 0:160, cols_o(g)], base[g])
        ring_o(g, j_in)
        send(part_o(g, j_in, x), part_o(g, j_in, x), base[g] + 2, pair, "o")
        rest = owb.at[j_in, 960:1000, cols_o(g)]
        send(rest, rest, base[g] + 2, pair, "o")

    def pair_o_half(g):
        arrived(owb.at[2, 0:80, cols_o(g)], base[g] + 1)
        for rows in half_o(zl):
            send(owb.at[2, rows, cols_o(g)], owb.at[2, rows, cols_o(g)], base[g] + 3, pair, "o")

    def own_o_out(g):
        arrived(owb.at[j_out, 0:160, cols_o(g)], base[g] + 2)
        ring_o(g, j_out)

    def own_o_half(g):
        arrived(owb.at[2, 0:80, cols_o(g)], base[g] + 3)
        ring_o(g, 2)

    def near_o(g, js=order):
        for j in js:
            arrived(owb.at[j, 0:240, cols_o(g)], base[g] + 3 + j)
            send(part_o(g, j, xl, 0, 64), part_o(g, j, xl, 0, 64), base[g] + 6 + j, right, "o")
            send(part_o(g, j, xr, 64, 56), part_o(g, j, xr, 64, 56), base[g] + 6 + j, left, "o")

    def far_o(g):
        for j in order:
            arrived(part_o(g, j, xf), base[g] + 6 + j)
            rows = pl.ds(pl.multiple_of(480 * c, 8), 480)
            send(owb.at[j, rows, cols_o(g)], owb.at[j, rows, cols_o(g)], base[g] + 10, sib, "o")

    def rows_w(start, size):
        return pl.ds(pl.multiple_of(128 * c + start, 16), size)

    def cols_w(g):
        lo, hi = SPAN[g]
        return slice(lo * 256, hi * 256)

    def part_w(g, j, q, start=0, size=32):
        return wb.at[j - 1, rows_w(64 * (q % 2) + 32 * (q // 2) + start, size), cols_w(g)]

    def block_in(g, j):
        return wb.at[j - 1, rows_w(64 * (x % 2), 64), cols_w(g)] if g in TWICE else part_w(g, j, x)

    def half_in(g, h):
        if g in TWICE:
            return wb.at[1, rows_w(64 * (x % 2) + 32 * h, 32), cols_w(g)]
        return part_w(g, 2, x, 16 * h, 16)

    def fetch(g):
        lo, hi = SPAN[g]
        unit = 64 if g in TWICE else 32
        first = 64 * (x % 2) + (0 if g in TWICE else 32 * (x // 2))
        for dev, zd, yd, j, start, size in (
            (near, zh + 2 * zl - 1, y + 2, j_out, 0, unit),
            (across, zh + 2, y, 2, unit // 2 * (1 - zl), unit // 2),
        ):
            rows = rows_w(first + start, size)
            k = lo
            while k < hi:
                dy, dz, half = TILES[k]
                wide = 512 if k == 6 else 256
                cols = pl.ds(pl.multiple_of(nid(zd + dz, yd + dy) * 512 + half * 256, 256), wide)
                sem = base[g] + (0 if size == unit else 1)
                send(w.at[rows, cols], wb.at[j - 1, rows, k * 256 : k * 256 + wide], sem, dev, "w")
                k += wide // 256

    def pair_w(g):
        arrived(block_in(g, j_in), base[g])
        send(block_in(g, j_in), block_in(g, j_in), base[g] + 2, pair, "w")
        arrived(half_in(g, zl), base[g] + 1)
        send(half_in(g, zl), half_in(g, zl), base[g] + 3, pair, "w")

    def ring_w(g, js=order):
        for j in js:
            if j is order[1]:
                arrived(block_in(g, j), base[g] + 2)
            elif j is order[2]:
                arrived(half_in(g, 1 - zl), base[g] + 3)
            send(part_w(g, j, x), part_w(g, j, x), base[g] + 3 + j, right, "w")
            send(part_w(g, j, x), part_w(g, j, x), base[g] + 3 + j, left, "w")

    def core_w(g):
        for j in order:
            arrived(wb.at[j - 1, 0:64, cols_w(g)], base[g] + 3 + j)
            half = wb.at[j - 1, rows_w(0, 128), cols_w(g)]
            send(half, half, base[g] + 7, sib, "w")

    def near_w(g, js=order):
        for j in js:
            arrived(wb.at[j - 1, 0:64, cols_w(g)], base[g] + 3 + j)
            send(part_w(g, j, xl, 0, 16), part_w(g, j, xl, 0, 16), base[g] + 6 + j, right, "w")
            send(part_w(g, j, xr, 16, 16), part_w(g, j, xr, 16, 16), base[g] + 6 + j, left, "w")

    def far_w(g):
        for j in order:
            arrived(part_w(g, j, xf), base[g] + 6 + j)
            half = wb.at[j - 1, rows_w(0, 128), cols_w(g)]
            send(half, half, base[g] + 10, sib, "w")

    def whole_w(g):
        arrived(wb.at[:, 0:128, cols_w(g)], base[g] + (7 if g in TWICE else 10))

    for g in "OP":
        fetch_o(g)
    for g in "OP":
        fetch_o_half(g)
    for dev in (right, far, left):
        send(cb.at[y, zh], ca.at[:, x, zl, c], cx, dev, "b")
    arrived(cb.at[0, 0:3], cz)
    for d in (1, 2, 3):
        send(cb.at[y], cb.at[y], cy + d - 1, (s, nid(zh, y + d)), "by")

    for i in range(4):
        wc[i].wait()

        def parts(k, _):
            cols = pl.ds(pl.multiple_of(k * 256, 256), 256)
            v = wl[:, cols]
            whl[0, :, cols], whl[1, :, cols] = split(v)
            ahl[0, :, cols], ahl[1, :, cols] = split(jnp.abs(v))
            return 0

        lax.fori_loop(8 * i, 8 * i + 8, parts, 0)
    ca[:, x, zl, c] = cb[y, zh]

    def pre_row(yy, carry):
        def body(k, carry):
            pc, pr = carry
            cols = pl.ds(pl.multiple_of((k * 4 + yy) * 512, 512), 512)
            chi, clo = split(cb[yy, k, 0])
            rhi, rlo = split(cb[yy, k, 1])
            cc, rr = jnp.concatenate([chi, clo], axis=0), jnp.concatenate([rhi, rlo], axis=0)
            pc = pc + dot_t(cc, whl[0, :, cols]) + dot_t(cc, whl[1, :, cols])
            pr = pr + dot_t(rr, ahl[0, :, cols]) + dot_t(rr, ahl[1, :, cols])
            return pc, pr

        return lax.fori_loop(0, 4, body, carry, unroll=True)

    zero = jnp.zeros((16, 256), F32)
    carry = pre_row(y, (zero, zero))
    pair_o_block("O")
    pair_o_block("P")
    fetch("A")
    pair_o_half("O")
    pair_o_half("P")
    def more(d, carry):
        arrived(cb.at[(y + 4 - d) % 4], cy + d - 1)
        return pre_row((y + 4 - d) % 4, carry)

    carry = more(1, carry)
    own_o_out("O")
    own_o_out("P")
    pair_w("A")
    ring_w("A", order[:1])
    fetch("B")
    own_o_half("O")
    own_o_half("P")
    carry = more(2, carry)
    carry = more(3, carry)
    pc = carry[0][0:8] + carry[0][8:16] + bias_v[...]
    pr = carry[1][0:8] + carry[1][8:16]
    upper, lower = pc + pr, pc - pr
    slope = jnp.clip(upper / (upper - lower), 0.0, 1.0)
    m = mask_v[...]
    sa[0, x, zl, c] = jnp.where(m == 1, 1.0, jnp.where(m == 2, slope, 0.0))
    sa[4, x, zl, c] = jnp.where(m == 2, slope * lower, 0.0)
    sj = take()
    for j in (1, 2, 3):
        dy, dz = CLASS[j]
        send(sa.at[0, x, zl, c], sa.at[j, x, zl, c], sj, (s, nid(zh - dz, y - dy)), "j")
    near_o("O", order[:2])
    near_o("P", order[:2])
    near_o("O", order[2:])
    near_o("P", order[2:])
    ring_w("A", order[1:])
    pair_w("B")
    fetch("C")
    fetch("D")
    arrived(sa.at[0:3, 0, 0, 0], sj)
    sx, sk = take(), take()
    for dev in others:
        send(sa.at[:, x, zl, c], sa.at[:, x, zl, c], sx, dev, "sx")
    cl, ck = take(), take()
    arrived(ca.at[:, 0:3, 0, 0], cx)
    send(ca.at[:, :, zl, c], ca.at[:, :, zl, c], cl, pair, "by")
    far_o("O")
    far_o("P")
    ring_w("B", order[:1])
    ring_w("B", order[1:])
    lc[2].wait()
    for g in "OP":
        arrived(owb.at[0:3, 0:480, cols_o(g)], base[g] + 10)

    def coeff(k, _):
        e = eb[...]
        for j in (2 * k, 2 * k + 1):
            hi, lo = split(owb[j])
            sc[j] = dot(e, hi) + dot(e, lo)
        return 0

    lax.fori_loop(0, 2, coeff, 0)

    arrived(owb.at[0, 0:280], sx)
    send(sa.at[:, :, :, c], sa.at[:, :, :, c], sk, sib, "s")
    core_w("A")
    core_w("B")
    pair_w("C")
    pair_w("D")
    ring_w("C", order[:1])
    arrived(sa.at[:, :, :, 1 - c], sk)

    def scale(k, _):
        o = ob[...]
        for j in (2 * k, 2 * k + 1):
            hi, lo = split(sa[j].reshape(128, 256))
            v = sc[j] * (dot(o, hi) + dot(o, lo))
            hi, lo = split(v)
            sh[j] = hi
            sl[j] = lo
        return 0

    lax.fori_loop(0, 2, scale, 0)
    rt = take(2)

    def prep(k):
        dy, dz, half = TILES[k]
        cols = pl.ds(pl.multiple_of(nid(zh + dz, y + dy) * 512 + half * 256, 256), 256)
        whi[k % 2, 0:256, :] = whl[0, :, cols]
        wlo[k % 2, 0:256, :] = whl[1, :, cols]
        for j in (1, 2, 3):
            hi, lo = split(wb[j - 1, :, k * 256 : k * 256 + 256])
            whi[k % 2, j * 256 : (j + 1) * 256, :] = hi
            wlo[k % 2, j * 256 : (j + 1) * 256, :] = lo

    def mul(k):
        a = jnp.concatenate([sh[j] for j in range(4)], axis=1)
        b = jnp.concatenate([sl[j] for j in range(4)], axis=1)
        for i in (0, 1):
            sendb[k + i] = dot(a, whi[i]) + dot(b, whi[i]) + dot(a, wlo[i])

    def pass_sum(k):
        dy, dz, half = TILES[k]
        send(sendb.at[k], recvb.at[SLOT[k]], rt + half, (s, nid(zh + dz, y + dy)), "r")

    whole_w("A")
    prep(0)
    prep(1)
    mul(0)
    pass_sum(0)
    pass_sum(1)
    ring_w("C", order[1:])
    whole_w("B")
    prep(2)
    prep(3)
    mul(2)
    pass_sum(2)
    pass_sum(3)
    near_w("C")
    arrived(ca.at[:, :, 1 - zl, c], cl)
    send(ca.at[:, :, :, c], ca.at[:, :, :, c], ck, sib, "bk")
    ring_w("D")
    far_w("C")
    whole_w("C")
    prep(4)
    prep(5)
    mul(4)
    pass_sum(4)
    pass_sum(5)
    hi, lo = split(sa[4].reshape(128, 256))
    off = dot(ob[...], hi) + dot(ob[...], lo)
    t = (sh[0].astype(F32) + sl[0].astype(F32)) * bias_v[...] - jnp.minimum(sc[0], 0.0) * off
    rel[...] = t[:, 0:128] + t[:, 128:256]
    near_w("D")
    arrived(ca.at[:, :, :, 1 - c], ck)
    for which, dst in ((0, crow), (1, rrow)):
        hi, lo = split(ca[which].reshape(128, 512))
        dst[...] = dot(ob[...], hi) + dot(ob[...], lo)
    far_w("D")
    whole_w("D")
    prep(6)
    prep(7)
    mul(6)

    written = []
    for half in (0, 1):
        cols = slice(half * 256, half * 256 + 256)
        arrived(recvb.at[0:3], rt + half)
        v = sendb[6 + half] + recvb[3 * half] + recvb[3 * half + 1] + recvb[3 * half + 2]
        outb[half] = v
        written.append(pltpu.make_async_copy(outb.at[half], out.at[:, cols], ls.at[half]))
        written[-1].start()
        t = v * crow[:, cols] - jnp.abs(v) * rrow[:, cols]
        rel[...] += t[:, 0:128] + t[:, 128:256]

    mb[n] = jnp.sum(jnp.transpose(rel[...]), axis=0, keepdims=True)
    ms = take()
    for d in range(1, 16):
        send(mb.at[n], mb.at[n], ms, (s, (n + d) % 16), "m")
    arrived(mb.at[0:15], ms)
    marg[...] = jnp.sum(mb[...], axis=0)

    for copy in written:
        copy.wait()
    for i, all_of_it in enumerate(kinds.values()):
        pltpu.make_async_copy(all_of_it, all_of_it, ss.at[i]).wait()


def finish(coeffs, margins, out, marg, held, row, sems):
    rows = [pl.ds(i * 128, 128) for i in range(4)]
    into = [pltpu.make_async_copy(coeffs.at[r], held.at[r], sems.at[i]) for i, r in enumerate(rows)]
    into.append(pltpu.make_async_copy(margins, row, sems.at[4]))
    back = [pltpu.make_async_copy(held.at[r], out.at[r], sems.at[5 + i]) for i, r in enumerate(rows)]
    back.append(pltpu.make_async_copy(row, marg, sems.at[9]))
    for copy in into:
        copy.start()
    for first, second in zip(into, back):
        first.wait()
        second.start()
    for copy in back:
        copy.wait()


def local(center, radius, weight, bias, out_weight, masks, image_labels, runner_up, spec_image):
    vmem, hbm = pl.BlockSpec(memory_space=pltpu.VMEM), pl.BlockSpec(memory_space=pl.ANY)
    coeffs, margins = pl.pallas_call(
        kernel,
        out_shape=(jax.ShapeDtypeStruct((512, 512), F32), jax.ShapeDtypeStruct((1, 512), F32)),
        in_specs=[hbm] * 9,
        out_specs=(hbm, vmem),
        scratch_shapes=[
            pltpu.VMEM((256, 8192), F32),
            pltpu.VMEM((2, 256, 8192), BF16),
            pltpu.VMEM((2, 256, 8192), BF16),
            pltpu.VMEM((3, 256, 2048), F32),
            pltpu.VMEM((4, 1024, 256), F32),
            pltpu.VMEM((4, 4, 2, 8, 512), F32),
            pltpu.VMEM((2, 4, 2, 2, 8, 512), F32),
            pltpu.VMEM((5, 4, 2, 2, 8, 256), F32),
            pltpu.VMEM((4, 512, 256), F32),
            pltpu.VMEM((4, 512, 256), BF16),
            pltpu.VMEM((4, 512, 256), BF16),
            pltpu.VMEM((2, 1024, 256), BF16),
            pltpu.VMEM((2, 1024, 256), BF16),
            pltpu.VMEM((8, 512, 256), F32),
            pltpu.VMEM((6, 512, 256), F32),
            pltpu.VMEM((2, 512, 256), F32),
            pltpu.VMEM((512, 512), F32),
            pltpu.VMEM((512, 512), F32),
            pltpu.VMEM((512, 128), F32),
            pltpu.VMEM((512, 1024), BF16),
            pltpu.VMEM((512, 128), BF16),
            pltpu.VMEM((16, 1, 512), F32),
            pltpu.VMEM((1, 256), F32),
            pltpu.VMEM((8, 256), jnp.int32),
            pltpu.VMEM((3, 512), jnp.int32),
            pltpu.SemaphoreType.DMA((10,)),
            pltpu.SemaphoreType.DMA((N_RECV,)),
            pltpu.SemaphoreType.DMA((12,)),
        ],
        compiler_params=pltpu.CompilerParams(
            collective_id=0, has_side_effects=True, vmem_limit_bytes=60 * 1024 * 1024
        ),
        name="bounds",
    )(
        center,
        radius,
        weight,
        bias.reshape(1, 256),
        out_weight,
        masks,
        image_labels.reshape(1, 128),
        runner_up.reshape(1, 512),
        spec_image.reshape(1, 512),
    )
    coeffs, margins = pl.pallas_call(
        finish,
        out_shape=(jax.ShapeDtypeStruct((512, 512), F32), jax.ShapeDtypeStruct((1, 512), F32)),
        in_specs=[hbm, hbm],
        out_specs=(hbm, hbm),
        scratch_shapes=[
            pltpu.VMEM((512, 512), F32),
            pltpu.VMEM((1, 512), F32),
            pltpu.SemaphoreType.DMA((10,)),
        ],
        name="finish",
    )(coeffs, margins)
    return coeffs, margins.reshape(512)


def solution(mesh):
    return jax.shard_map(
        local,
        mesh=mesh,
        in_specs=(
            P("spec", "neuron"),
            P("spec", "neuron"),
            P("neuron", None),
            P("neuron"),
            P(None, "neuron"),
            P(None, "neuron"),
            P(),
            P("spec"),
            P("spec"),
        ),
        out_specs=(P("spec", "neuron"), P("spec")),
        check_vma=False,
    )
```

```python
import jax
import jax.numpy as jnp
from jax import lax
from jax.experimental import pallas as pl
from jax.experimental.pallas import tpu as pltpu
from jax.sharding import PartitionSpec as P

MESH = pl.DeviceIdType.MESH
F32, BF16 = jnp.float32, jnp.bfloat16


def split(v):
    hi = v.astype(BF16)
    return hi, (v - hi.astype(F32)).astype(BF16)


def dot(a, b):
    return lax.dot_general(a, b, (((1,), (0,)), ((), ())), preferred_element_type=F32)


def dot_t(a, b):
    return lax.dot_general(a, b, (((1,), (1,)), ((), ())), preferred_element_type=F32)


def sid(x, zl, c):
    return ((x + 4) % 4 * 2 + zl) * 2 + c


def nid(zh, y):
    return (zh + 4) % 4 * 4 + (y + 4) % 4


TILES = ((1, 0, 0), (-1, 0, 0), (0, 1, 0), (0, -1, 1), (1, 0, 1), (-1, 0, 1), (0, 0, 0), (0, 0, 1))
SLOT = (0, 1, 2, 3, 4, 5)
TWICE = "AB"
SPAN = {"A": (0, 2), "B": (2, 4), "C": (4, 6), "D": (6, 8)}
CLASS = ((0, 0), (2, 1), (0, 2), (2, 3))
N_RECV = 73


def kernel(
    center, radius, w, bias, ow, masks, labels, runner, simg, out, marg,
    wl, whl, ahl, wb, owb, cb, ca, sa, sc, sh, sl, whi, wlo, sendb, recvb, outb, crow, rrow, rel, eb, ob, mb,
    bias_v, mask_v, ids_v, ss, rs, ls,
):
    s, n = lax.axis_index("spec"), lax.axis_index("neuron")
    x, zl, c = s // 4, s // 2 % 2, s % 2
    zh, y = n // 4, n % 4

    counter = [0]
    kinds = {
        "o": owb.at[0:3, 0:1000],
        "w": wb,
        "b": cb.at[0:3, 0:2],
        "by": cb,
        "bk": cb.at[0:2],
        "j": sa.at[0:3, 0, 0, 0],
        "sx": owb.at[0, 0:280],
        "s": sa.at[:, 0:2],
        "r": recvb,
        "m": mb.at[0:15],
    }

    def take(k=1):
        counter[0] += k
        assert counter[0] <= N_RECV
        return counter[0] - k

    def send(src, dst, sem, dev, kind):
        pltpu.make_async_remote_copy(
            src_ref=src, dst_ref=dst, send_sem=ss.at[list(kinds).index(kind)], recv_sem=rs.at[sem],
            device_id=dev, device_id_type=MESH,
        ).start()

    def arrived(dst, sem):
        pltpu.make_async_copy(dst, dst, rs.at[sem]).wait()

    lc = [
        pltpu.make_async_copy(center, cb.at[y, zh, 0], ls.at[0]),
        pltpu.make_async_copy(radius, cb.at[y, zh, 1], ls.at[1]),
        pltpu.make_async_copy(ow, owb.at[0, 0:1000], ls.at[2]),
    ]
    small = [
        pltpu.make_async_copy(bias, bias_v, ls.at[7]),
        pltpu.make_async_copy(masks.at[pl.ds(pl.multiple_of(8 * s, 8), 8)], mask_v, ls.at[8]),
        pltpu.make_async_copy(labels, ids_v.at[0:1, 0:128], ls.at[9]),
        pltpu.make_async_copy(runner, ids_v.at[1:2], ls.at[10]),
        pltpu.make_async_copy(simg, ids_v.at[2:3], ls.at[11]),
    ]
    wc = [
        pltpu.make_async_copy(w.at[:, pl.ds(i * 2048, 2048)], wl.at[:, pl.ds(i * 2048, 2048)], ls.at[3 + i])
        for i in range(4)
    ]
    for copy in lc[:2] + small:
        copy.start()

    right, left, far = (sid(x + 1, zl, c), n), (sid(x - 1, zl, c), n), (sid(x + 2, zl, c), n)
    pair, sib = (sid(x, 1 - zl, c), n), (sid(x, zl, 1 - c), n)
    near = (sid(x, 1 - zl, c), nid(zh + 2 * zl - 1, y + 2))
    across = (sid(x, 1 - zl, c), nid(zh + 2, y))
    others = [(sid(x + d, zl + e - 2 * zl * e, c), n) for d in range(4) for e in (0, 1) if d or e]
    peers = [(s, (n + d) % 16) for d in range(1, 16)] + others + [sib, near, across]
    barrier = pltpu.get_barrier_semaphore()
    for peer in peers:
        pl.semaphore_signal(barrier, inc=1, device_id=peer, device_id_type=MESH)
    for copy in wc + lc[2:]:
        copy.start()
    for copy in small:
        copy.wait()
    img = jnp.transpose(jnp.broadcast_to(ids_v[2:3], (128, 512)))
    run = jnp.transpose(jnp.broadcast_to(ids_v[1:2], (128, 512)))[:, 0:1]
    picked = img == lax.broadcasted_iota(jnp.int32, (512, 128), 1)
    ob[...] = jnp.where(picked, 1.0, 0.0).astype(BF16)
    label = ids_v[0:1, 0:128].astype(F32)
    lab = jnp.sum(jnp.where(picked, label, 0.0), axis=1, keepdims=True).astype(jnp.int32)
    for k in range(8):
        ids = lax.broadcasted_iota(jnp.int32, (512, 128), 1) + k * 128
        e = jnp.where(ids == lab, 1.0, 0.0) - jnp.where(ids == run, 1.0, 0.0)
        eb[:, k * 128 : (k + 1) * 128] = e.astype(BF16)
    for j in range(4):
        owb[j, 1000:1024, :] = jnp.zeros((24, 256), F32)
    pl.semaphore_wait(barrier, len(peers))

    lc[0].wait()
    lc[1].wait()
    cz, cy, cx = take(), take(3), take()
    for d in (1, 2, 3):
        send(cb.at[y, zh], cb.at[y, zh], cz, (s, nid(zh + d, y)), "b")

    j_in, j_out = 3 - 2 * zl, 1 + 2 * zl
    order = (j_in, j_out, 2)
    base = {g: take(8 if g in TWICE else 11) for g in "OPABCD"}
    xl, xr, xf = (x + 3) % 4, (x + 1) % 4, (x + 2) % 4

    def part_o(g, j, q, start=0, size=120):
        rows = pl.ds(pl.multiple_of(480 * c + 120 * q + start, 8), size)
        return owb.at[j, rows, cols_o(g)]

    def cols_o(g):
        return slice(0, 128) if g == "O" else slice(128, 256)

    def half_o(h):
        start = 480 * c + 120 * x
        first = pl.ds(pl.multiple_of(start + 80 * h, 8), 40)
        second = pl.ds(pl.multiple_of(jnp.where(h == 0, start + 40, 960), 8), 40)
        return first, second

    def fetch_o(g):
        for rows in (pl.ds(pl.multiple_of(480 * c + 120 * x, 8), 120), slice(960, 1000)):
            send(ow.at[rows, cols_o(g)], owb.at[j_out, rows, cols_o(g)], base[g], near, "o")

    def fetch_o_half(g):
        for rows in half_o(1 - zl):
            send(ow.at[rows, cols_o(g)], owb.at[2, rows, cols_o(g)], base[g] + 1, across, "o")

    def ring_o(g, j):
        send(part_o(g, j, x), part_o(g, j, x), base[g] + 3 + j, right, "o")
        send(part_o(g, j, x), part_o(g, j, x), base[g] + 3 + j, left, "o")

    def pair_o_block(g):
        arrived(owb.at[j_in, 0:160, cols_o(g)], base[g])
        ring_o(g, j_in)
        send(part_o(g, j_in, x), part_o(g, j_in, x), base[g] + 2, pair, "o")
        rest = owb.at[j_in, 960:1000, cols_o(g)]
        send(rest, rest, base[g] + 2, pair, "o")

    def pair_o_half(g):
        arrived(owb.at[2, 0:80, cols_o(g)], base[g] + 1)
        for rows in half_o(zl):
            send(owb.at[2, rows, cols_o(g)], owb.at[2, rows, cols_o(g)], base[g] + 3, pair, "o")

    def own_o_out(g):
        arrived(owb.at[j_out, 0:160, cols_o(g)], base[g] + 2)
        ring_o(g, j_out)

    def own_o_half(g):
        arrived(owb.at[2, 0:80, cols_o(g)], base[g] + 3)
        ring_o(g, 2)

    def near_o(g, js=order):
        for j in js:
            arrived(owb.at[j, 0:240, cols_o(g)], base[g] + 3 + j)
            send(part_o(g, j, xl, 0, 64), part_o(g, j, xl, 0, 64), base[g] + 6 + j, right, "o")
            send(part_o(g, j, xr, 64, 56), part_o(g, j, xr, 64, 56), base[g] + 6 + j, left, "o")

    def far_o(g):
        for j in order:
            arrived(part_o(g, j, xf), base[g] + 6 + j)
            rows = pl.ds(pl.multiple_of(480 * c, 8), 480)
            send(owb.at[j, rows, cols_o(g)], owb.at[j, rows, cols_o(g)], base[g] + 10, sib, "o")

    def rows_w(start, size):
        return pl.ds(pl.multiple_of(128 * c + start, 16), size)

    def cols_w(g):
        lo, hi = SPAN[g]
        return slice(lo * 256, hi * 256)

    def part_w(g, j, q, start=0, size=32):
        return wb.at[j - 1, rows_w(64 * (q % 2) + 32 * (q // 2) + start, size), cols_w(g)]

    def block_in(g, j):
        return wb.at[j - 1, rows_w(64 * (x % 2), 64), cols_w(g)] if g in TWICE else part_w(g, j, x)

    def half_in(g, h):
        if g in TWICE:
            return wb.at[1, rows_w(64 * (x % 2) + 32 * h, 32), cols_w(g)]
        return part_w(g, 2, x, 16 * h, 16)

    def fetch(g):
        lo, hi = SPAN[g]
        unit = 64 if g in TWICE else 32
        first = 64 * (x % 2) + (0 if g in TWICE else 32 * (x // 2))
        for dev, zd, yd, j, start, size in (
            (near, zh + 2 * zl - 1, y + 2, j_out, 0, unit),
            (across, zh + 2, y, 2, unit // 2 * (1 - zl), unit // 2),
        ):
            rows = rows_w(first + start, size)
            k = lo
            while k < hi:
                dy, dz, half = TILES[k]
                wide = 512 if k == 6 else 256
                cols = pl.ds(pl.multiple_of(nid(zd + dz, yd + dy) * 512 + half * 256, 256), wide)
                sem = base[g] + (0 if size == unit else 1)
                send(w.at[rows, cols], wb.at[j - 1, rows, k * 256 : k * 256 + wide], sem, dev, "w")
                k += wide // 256

    def pair_w(g):
        arrived(block_in(g, j_in), base[g])
        send(block_in(g, j_in), block_in(g, j_in), base[g] + 2, pair, "w")
        arrived(half_in(g, zl), base[g] + 1)
        send(half_in(g, zl), half_in(g, zl), base[g] + 3, pair, "w")

    def ring_w(g, js=order):
        for j in js:
            if j is order[1]:
                arrived(block_in(g, j), base[g] + 2)
            elif j is order[2]:
                arrived(half_in(g, 1 - zl), base[g] + 3)
            send(part_w(g, j, x), part_w(g, j, x), base[g] + 3 + j, right, "w")
            send(part_w(g, j, x), part_w(g, j, x), base[g] + 3 + j, left, "w")

    def core_w(g):
        for j in order:
            arrived(wb.at[j - 1, 0:64, cols_w(g)], base[g] + 3 + j)
            half = wb.at[j - 1, rows_w(0, 128), cols_w(g)]
            send(half, half, base[g] + 7, sib, "w")

    def near_w(g, js=order):
        for j in js:
            arrived(wb.at[j - 1, 0:64, cols_w(g)], base[g] + 3 + j)
            send(part_w(g, j, xl, 0, 16), part_w(g, j, xl, 0, 16), base[g] + 6 + j, right, "w")
            send(part_w(g, j, xr, 16, 16), part_w(g, j, xr, 16, 16), base[g] + 6 + j, left, "w")

    def far_w(g):
        for j in order:
            arrived(part_w(g, j, xf), base[g] + 6 + j)
            half = wb.at[j - 1, rows_w(0, 128), cols_w(g)]
            send(half, half, base[g] + 10, sib, "w")

    def whole_w(g):
        arrived(wb.at[:, 0:128, cols_w(g)], base[g] + (7 if g in TWICE else 10))

    for g in "OP":
        fetch_o(g)
    for g in "OP":
        fetch_o_half(g)
    for dev in (right, far, left):
        send(cb.at[y, zh], ca.at[:, x, zl, c], cx, dev, "b")
    arrived(cb.at[0, 0:3], cz)
    for d in (1, 2, 3):
        send(cb.at[y], cb.at[y], cy + d - 1, (s, nid(zh, y + d)), "by")

    for i in range(4):
        wc[i].wait()

        def parts(k, _):
            cols = pl.ds(pl.multiple_of(k * 256, 256), 256)
            v = wl[:, cols]
            whl[0, :, cols], whl[1, :, cols] = split(v)
            ahl[0, :, cols], ahl[1, :, cols] = split(jnp.abs(v))
            return 0

        lax.fori_loop(8 * i, 8 * i + 8, parts, 0)
    ca[:, x, zl, c] = cb[y, zh]

    def pre_row(yy, carry):
        def body(k, carry):
            pc, pr = carry
            cols = pl.ds(pl.multiple_of((k * 4 + yy) * 512, 512), 512)
            chi, clo = split(cb[yy, k, 0])
            rhi, rlo = split(cb[yy, k, 1])
            cc, rr = jnp.concatenate([chi, clo], axis=0), jnp.concatenate([rhi, rlo], axis=0)
            pc = pc + dot_t(cc, whl[0, :, cols]) + dot_t(cc, whl[1, :, cols])
            pr = pr + dot_t(rr, ahl[0, :, cols]) + dot_t(rr, ahl[1, :, cols])
            return pc, pr

        return lax.fori_loop(0, 4, body, carry, unroll=True)

    zero = jnp.zeros((16, 256), F32)
    carry = pre_row(y, (zero, zero))
    pair_o_block("O")
    pair_o_block("P")
    fetch("A")
    pair_o_half("O")
    pair_o_half("P")
    def more(d, carry):
        arrived(cb.at[(y + 4 - d) % 4], cy + d - 1)
        return pre_row((y + 4 - d) % 4, carry)

    carry = more(1, carry)
    own_o_out("O")
    own_o_out("P")
    pair_w("A")
    ring_w("A", order[:1])
    fetch("B")
    own_o_half("O")
    own_o_half("P")
    carry = more(2, carry)
    carry = more(3, carry)
    pc = carry[0][0:8] + carry[0][8:16] + bias_v[...]
    pr = carry[1][0:8] + carry[1][8:16]
    upper, lower = pc + pr, pc - pr
    slope = jnp.clip(upper / (upper - lower), 0.0, 1.0)
    m = mask_v[...]
    sa[0, x, zl, c] = jnp.where(m == 1, 1.0, jnp.where(m == 2, slope, 0.0))
    sa[4, x, zl, c] = jnp.where(m == 2, slope * lower, 0.0)
    sj = take()
    for j in (1, 2, 3):
        dy, dz = CLASS[j]
        send(sa.at[0, x, zl, c], sa.at[j, x, zl, c], sj, (s, nid(zh - dz, y - dy)), "j")
    near_o("O", order[:2])
    near_o("P", order[:2])
    near_o("O", order[2:])
    near_o("P", order[2:])
    ring_w("A", order[1:])
    pair_w("B")
    fetch("C")
    fetch("D")
    arrived(sa.at[0:3, 0, 0, 0], sj)
    sx, sk = take(), take()
    for dev in others:
        send(sa.at[:, x, zl, c], sa.at[:, x, zl, c], sx, dev, "sx")
    cl, ck = take(), take()
    arrived(ca.at[:, 0:3, 0, 0], cx)
    send(ca.at[:, :, zl, c], ca.at[:, :, zl, c], cl, pair, "by")
    far_o("O")
    far_o("P")
    ring_w("B", order[:1])
    ring_w("B", order[1:])
    lc[2].wait()
    for g in "OP":
        arrived(owb.at[0:3, 0:480, cols_o(g)], base[g] + 10)

    def coeff(k, _):
        e = eb[...]
        for j in (2 * k, 2 * k + 1):
            hi, lo = split(owb[j])
            sc[j] = dot(e, hi) + dot(e, lo)
        return 0

    lax.fori_loop(0, 2, coeff, 0)

    arrived(owb.at[0, 0:280], sx)
    send(sa.at[:, :, :, c], sa.at[:, :, :, c], sk, sib, "s")
    core_w("A")
    core_w("B")
    pair_w("C")
    pair_w("D")
    ring_w("C", order[:1])
    arrived(sa.at[:, :, :, 1 - c], sk)

    def scale(k, _):
        o = ob[...]
        for j in (2 * k, 2 * k + 1):
            hi, lo = split(sa[j].reshape(128, 256))
            v = sc[j] * (dot(o, hi) + dot(o, lo))
            hi, lo = split(v)
            sh[j] = hi
            sl[j] = lo
        return 0

    lax.fori_loop(0, 2, scale, 0)
    rt = take(2)

    def prep(k):
        dy, dz, half = TILES[k]
        cols = pl.ds(pl.multiple_of(nid(zh + dz, y + dy) * 512 + half * 256, 256), 256)
        whi[k % 2, 0:256, :] = whl[0, :, cols]
        wlo[k % 2, 0:256, :] = whl[1, :, cols]
        for j in (1, 2, 3):
            hi, lo = split(wb[j - 1, :, k * 256 : k * 256 + 256])
            whi[k % 2, j * 256 : (j + 1) * 256, :] = hi
            wlo[k % 2, j * 256 : (j + 1) * 256, :] = lo

    def mul(k):
        a = jnp.concatenate([sh[j] for j in range(4)], axis=1)
        b = jnp.concatenate([sl[j] for j in range(4)], axis=1)
        for i in (0, 1):
            sendb[k + i] = dot(a, whi[i]) + dot(b, whi[i]) + dot(a, wlo[i])

    def pass_sum(k):
        dy, dz, half = TILES[k]
        send(sendb.at[k], recvb.at[SLOT[k]], rt + half, (s, nid(zh + dz, y + dy)), "r")

    whole_w("A")
    prep(0)
    prep(1)
    mul(0)
    pass_sum(0)
    pass_sum(1)
    ring_w("C", order[1:])
    whole_w("B")
    prep(2)
    prep(3)
    mul(2)
    pass_sum(2)
    pass_sum(3)
    near_w("C")
    arrived(ca.at[:, :, 1 - zl, c], cl)
    send(ca.at[:, :, :, c], ca.at[:, :, :, c], ck, sib, "bk")
    ring_w("D")
    far_w("C")
    whole_w("C")
    prep(4)
    prep(5)
    mul(4)
    pass_sum(4)
    pass_sum(5)
    hi, lo = split(sa[4].reshape(128, 256))
    off = dot(ob[...], hi) + dot(ob[...], lo)
    t = (sh[0].astype(F32) + sl[0].astype(F32)) * bias_v[...] - jnp.minimum(sc[0], 0.0) * off
    rel[...] = t[:, 0:128] + t[:, 128:256]
    near_w("D")
    arrived(ca.at[:, :, :, 1 - c], ck)
    for which, dst in ((0, crow), (1, rrow)):
        hi, lo = split(ca[which].reshape(128, 512))
        dst[...] = dot(ob[...], hi) + dot(ob[...], lo)
    far_w("D")
    whole_w("D")
    prep(6)
    prep(7)
    mul(6)

    written = []
    for half in (0, 1):
        cols = slice(half * 256, half * 256 + 256)
        arrived(recvb.at[0:3], rt + half)
        v = sendb[6 + half] + recvb[3 * half] + recvb[3 * half + 1] + recvb[3 * half + 2]
        outb[half] = v
        written.append(pltpu.make_async_copy(outb.at[half], out.at[:, cols], ls.at[half]))
        written[-1].start()
        t = v * crow[:, cols] - jnp.abs(v) * rrow[:, cols]
        rel[...] += t[:, 0:128] + t[:, 128:256]

    mb[n] = jnp.sum(jnp.transpose(rel[...]), axis=0, keepdims=True)
    ms = take()
    for dz, dy in [(dz, dy) for dz in (2, 1, 3, 0) for dy in (2, 1, 3, 0) if dz or dy]:
        send(mb.at[n], mb.at[n], ms, (s, nid(zh + dz, y + dy)), "m")
    arrived(mb.at[0:15], ms)
    marg[...] = jnp.sum(mb[...], axis=0)

    for copy in written:
        copy.wait()
    for i, all_of_it in enumerate(kinds.values()):
        pltpu.make_async_copy(all_of_it, all_of_it, ss.at[i]).wait()


def finish(coeffs, margins, out, marg, held, row, sems):
    rows = [pl.ds(i * 128, 128) for i in range(4)]
    into = [pltpu.make_async_copy(coeffs.at[r], held.at[r], sems.at[i]) for i, r in enumerate(rows)]
    into.append(pltpu.make_async_copy(margins, row, sems.at[4]))
    back = [pltpu.make_async_copy(held.at[r], out.at[r], sems.at[5 + i]) for i, r in enumerate(rows)]
    back.append(pltpu.make_async_copy(row, marg, sems.at[9]))
    for copy in into:
        copy.start()
    for first, second in zip(into, back):
        first.wait()
        second.start()
    for copy in back:
        copy.wait()


def local(center, radius, weight, bias, out_weight, masks, image_labels, runner_up, spec_image):
    vmem, hbm = pl.BlockSpec(memory_space=pltpu.VMEM), pl.BlockSpec(memory_space=pl.ANY)
    coeffs, margins = pl.pallas_call(
        kernel,
        out_shape=(jax.ShapeDtypeStruct((512, 512), F32), jax.ShapeDtypeStruct((1, 512), F32)),
        in_specs=[hbm] * 9,
        out_specs=(hbm, vmem),
        scratch_shapes=[
            pltpu.VMEM((256, 8192), F32),
            pltpu.VMEM((2, 256, 8192), BF16),
            pltpu.VMEM((2, 256, 8192), BF16),
            pltpu.VMEM((3, 256, 2048), F32),
            pltpu.VMEM((4, 1024, 256), F32),
            pltpu.VMEM((4, 4, 2, 8, 512), F32),
            pltpu.VMEM((2, 4, 2, 2, 8, 512), F32),
            pltpu.VMEM((5, 4, 2, 2, 8, 256), F32),
            pltpu.VMEM((4, 512, 256), F32),
            pltpu.VMEM((4, 512, 256), BF16),
            pltpu.VMEM((4, 512, 256), BF16),
            pltpu.VMEM((2, 1024, 256), BF16),
            pltpu.VMEM((2, 1024, 256), BF16),
            pltpu.VMEM((8, 512, 256), F32),
            pltpu.VMEM((6, 512, 256), F32),
            pltpu.VMEM((2, 512, 256), F32),
            pltpu.VMEM((512, 512), F32),
            pltpu.VMEM((512, 512), F32),
            pltpu.VMEM((512, 128), F32),
            pltpu.VMEM((512, 1024), BF16),
            pltpu.VMEM((512, 128), BF16),
            pltpu.VMEM((16, 1, 512), F32),
            pltpu.VMEM((1, 256), F32),
            pltpu.VMEM((8, 256), jnp.int32),
            pltpu.VMEM((3, 512), jnp.int32),
            pltpu.SemaphoreType.DMA((10,)),
            pltpu.SemaphoreType.DMA((N_RECV,)),
            pltpu.SemaphoreType.DMA((12,)),
        ],
        compiler_params=pltpu.CompilerParams(
            collective_id=0, has_side_effects=True, vmem_limit_bytes=60 * 1024 * 1024
        ),
        name="bounds",
    )(
        center,
        radius,
        weight,
        bias.reshape(1, 256),
        out_weight,
        masks,
        image_labels.reshape(1, 128),
        runner_up.reshape(1, 512),
        spec_image.reshape(1, 512),
    )
    coeffs, margins = pl.pallas_call(
        finish,
        out_shape=(jax.ShapeDtypeStruct((512, 512), F32), jax.ShapeDtypeStruct((1, 512), F32)),
        in_specs=[hbm, hbm],
        out_specs=(hbm, hbm),
        scratch_shapes=[
            pltpu.VMEM((512, 512), F32),
            pltpu.VMEM((1, 512), F32),
            pltpu.SemaphoreType.DMA((10,)),
        ],
        name="finish",
    )(coeffs, margins)
    return coeffs, margins.reshape(512)


def solution(mesh):
    return jax.shard_map(
        local,
        mesh=mesh,
        in_specs=(
            P("spec", "neuron"),
            P("spec", "neuron"),
            P("neuron", None),
            P("neuron"),
            P(None, "neuron"),
            P(None, "neuron"),
            P(),
            P("spec"),
            P("spec"),
        ),
        out_specs=(P("spec", "neuron"), P("spec")),
        check_vma=False,
    )
```
